32 devices in a mesh: pairs: 8 (over y, x, core), fit: 4 (over z).
Axes of the slice: x: 2, y: 2, z: 4, core: 2. Of those that a mesh axis runs over, the one named last changes fastest.
Arguments:
- b_first: bfloat16 [64, 160, 3072], P('pairs', None, 'fit'), may hold values from -0.109375 to 0.109375
- b_second: bfloat16 [64, 160, 3072], P('pairs', None, 'fit'), may hold values from -6 to 6
- start_amplitudes: float32 [64, 160, 160], P('pairs'), may hold values from -1.8 to 1.8
- margins: bfloat16 [64, 96, 160, 160], P('pairs', 'fit'), may hold values from -0.5 to 0.5
- fock_terms: float32 [64, 96], P('pairs', 'fit'), may hold values from -0.2 to 0.2
- partners: int32 [64, 96], P('pairs', 'fit'), may hold values from 0 to 63, as said below
- pno_energy: float32 [64, 160], P('pairs'), may hold values from 0.3 to 1.5
- occ_energy: float32 [4000], replicated, may hold values from -1 to -0.2
- pair_list: int32 [64, 2], P('pairs'), may hold values from 0 to 3999
- pno_count: int32 [64], P('pairs'), may hold values from 64 to 160, as said below
Outputs:
- amplitudes: float32 [64, 160, 160], P('pairs')
- residual: float32 [64, 160, 160], P('pairs')
The draws below stay inside these ranges and needn't reach their ends.
Inputs may be any that keep to these rules, and one draw needn't show every extreme that they name: `pno_count`: each pair's PNO count is one of 64, 128 and 160. `partners`: pairs owner * 8 to owner * 8 + 7 belong to one owner. In the block of one device (its 8 rows and the columns of its index along fit), each owner's pairs appear at most 48 times, and one owner's pairs appear exactly 48 times in every block.
All inputs are finite; a program needn't handle non-finite values.
Results may differ from the reference program's by a relative error of at most 0.0041.
Values may be sent and summed in bfloat16 or wider, within the bound.
A program may use at most 192 MiB of HBM per device.

```python
from functools import partial
import jax
import jax.numpy as jnp
from jax import lax

NPNO = 160
FIT = 3072
NOCC = 4000
PARTNERS = 96
ITERS = 2
PAIR_DEV = 8
PAIRS = 64
N_PAIRS = 8
N_FIT = 4


def block_partners(common_owner, key):
    order_key, pick_key, local_key = jax.random.split(key, 3)
    request_count = PAIR_DEV * PARTNERS // N_FIT
    capacity = 2 * request_count // N_PAIRS
    slot_owner = jnp.arange(N_PAIRS * capacity, dtype=jnp.int32) // capacity
    rotated = (slot_owner + common_owner) % N_PAIRS
    remaining = jax.random.permutation(order_key, rotated[capacity:])
    chosen = jnp.concatenate([rotated[:capacity], remaining])[:request_count]
    chosen = jax.random.permutation(pick_key, chosen)
    local_index = jax.random.randint(local_key, (request_count,), 0, PAIR_DEV)
    return (chosen * PAIR_DEV + local_index).reshape(PAIR_DEV, PARTNERS // N_FIT)


def draw_partners(key, part):
    common_owner = jax.random.randint(jax.random.fold_in(key, 7), (), 0, N_PAIRS)
    block_keys = jax.random.split(jax.random.fold_in(key, 11), N_PAIRS * N_FIT)
    blocks = jax.vmap(lambda single: block_partners(common_owner, single))(block_keys)
    blocks = blocks.reshape(N_PAIRS, N_FIT, PAIR_DEV, PARTNERS // N_FIT)
    return jnp.transpose(blocks, (0, 2, 1, 3)).reshape(PAIRS, PARTNERS).astype(jnp.int32)


def draw_pno_count(key, part):
    level_index = jax.random.randint(jax.random.fold_in(key, 3), (PAIRS,), 0, 3)
    level_table = jnp.array([NPNO * 2 // 5, NPNO * 4 // 5, NPNO], dtype=jnp.int32)
    return level_table[level_index]


def touch_ends(result, own_key, least, largest):
    index_at = [jax.random.randint(jax.random.fold_in(own_key, axis), (), 0, length) for axis, length in enumerate(result.shape)]
    longest = result.shape.index(max(result.shape))
    next_to = index_at[:longest] + [(index_at[longest] + 1) % result.shape[longest]] + index_at[longest + 1:]
    return result.at[tuple(index_at)].set(least).at[tuple(next_to)].set(largest)


def level_of(rng, extent, shards, least, largest):
    factor_of = 1.0
    for position, parts in shards:
        draws = jax.random.uniform(jax.random.fold_in(jax.random.fold_in(rng, 6), position), (parts,), jnp.float32, least / len(shards), largest / len(shards))
        factor_of = factor_of * jnp.repeat(jnp.exp(draws), extent[position] // parts).reshape((-1,) + (1,) * (len(extent) - 1 - position))
    return factor_of


def bell_draw(key, shape, scale, reach, cuts=(), held_as=jnp.bfloat16):
    loudness = level_of(key, shape, cuts, -0.22, 0.18) if cuts else 1.0
    entries = jax.random.normal(key, shape, jnp.float32) * scale * loudness
    return jnp.minimum(jnp.maximum(entries, -reach), reach).astype(held_as)


def setup_inputs(seed: int = 0) -> dict:
    splits = jax.random.split(jax.random.key(seed), 11)
    return {
        "b_first": bell_draw(splits[0], (PAIRS, NPNO, FIT), FIT ** -0.5, 0.109375, ((0, 8), (2, 4))),
        "b_second": bell_draw(splits[1], (PAIRS, NPNO, FIT), 1.0, 6.0, ((0, 8), (2, 4))),
        "start_amplitudes": bell_draw(splits[2], (PAIRS, NPNO, NPNO), 0.3, 1.8, ((0, 8),), jnp.float32),
        "margins": bell_draw(splits[3], (PAIRS, PARTNERS, NPNO, NPNO), NPNO ** -0.5, 0.5, ((0, 8), (1, 4))),
        "fock_terms": jnp.clip(jax.random.uniform(splits[4], (PAIRS, PARTNERS), jnp.float32, -0.2, 0.2) * level_of(splits[4], (PAIRS, PARTNERS), ((0, 8), (1, 4)), -0.4, 0.0), -0.2, 0.2),
        "partners": draw_partners(jax.random.fold_in(splits[10], 71), 0),
        "pno_energy": jnp.clip(0.3 + 1.2 * jax.random.uniform(splits[6], (PAIRS, NPNO), jnp.float32) ** level_of(splits[6], (PAIRS, NPNO), ((0, 8),), -0.2, 0.2), 0.3, 1.5),
        "occ_energy": jnp.clip(jax.random.uniform(splits[7], (NOCC,), jnp.float32, -1.0, -0.2), -1.0, -0.2),
        "pair_list": touch_ends(jax.random.randint(splits[8], (PAIRS, 2), 0, NOCC), jax.random.fold_in(splits[8], 1), 0, NOCC - 1).astype(jnp.int32),
        "pno_count": draw_pno_count(jax.random.fold_in(splits[10], 71), 0),
    }


def pair_coupling(rounded, pieces):
    margin_rows, fock_row, partner_row = pieces
    fetched = rounded[partner_row].astype(jnp.float32)
    margin_block = margin_rows.astype(jnp.float32)
    left_product = jnp.einsum("pac,pcd->pad", margin_block, fetched, precision=lax.Precision.HIGHEST)
    left_product = lax.optimization_barrier(left_product.astype(jnp.bfloat16)).astype(jnp.float32)
    right_product = jnp.einsum("pad,pbd->pab", left_product, margin_block, precision=lax.Precision.HIGHEST)
    return jnp.sum(fock_row[:, None, None] * right_product, axis=0)


def pair_integrals(pieces):
    return jnp.dot(pieces[0], pieces[1].T, preferred_element_type=jnp.float32)


def reference(b_first, b_second, start_amplitudes, margins, fock_terms, partners, pno_energy, occ_energy, pair_list, pno_count):
    levels = jnp.arange(NPNO, dtype=jnp.int32)
    keep_rows = (levels[None, :] < pno_count[:, None]).astype(jnp.float32)
    pair_mask = keep_rows[:, :, None] * keep_rows[:, None, :]
    occ_pair = occ_energy[pair_list[:, 0]] + occ_energy[pair_list[:, 1]]
    denominator = pno_energy[:, :, None] + pno_energy[:, None, :] - occ_pair[:, None, None]
    integrals = lax.map(pair_integrals, (b_first, b_second))
    amplitudes = pair_mask * start_amplitudes
    residual = jnp.zeros_like(amplitudes)
    for iteration in range(ITERS):
        rounded = amplitudes.astype(jnp.bfloat16)
        coupling = lax.map(partial(pair_coupling, rounded), (margins, fock_terms, partners))
        residual = pair_mask * (integrals - coupling + denominator * amplitudes)
        amplitudes = amplitudes - residual / denominator
    return amplitudes, residual
```

```python
import functools
import jax
import jax.numpy as jnp
from jax import lax
from jax.experimental import pallas as pl
from jax.experimental.pallas import tpu as pltpu
from jax.sharding import PartitionSpec as P

ITERS = 2
LANES = 128
SUBLANES = 16
REDUCE_LAG = 2
SPREAD_LAG = 5
BF16 = jnp.bfloat16
F32 = jnp.float32


def flip(value, bits, size):
    result, place = 0, 1
    while place < size:
        one = (value // place) % 2
        other = (bits // place) % 2
        result = result + place * ((one + other) % 2)
        place *= 2
    return result


def tail_shape(width):
    tail = width - LANES
    fold = LANES // tail
    rows = -(-width // (fold * SUBLANES)) * SUBLANES
    return tail, fold, rows


def kernel(
    n_pairs,
    n_fit,
    start_ref,
    energy_ref,
    fock_ref,
    partner_ref,
    occ_ref,
    list_ref,
    count_ref,
    b_first_ref,
    b_second_ref,
    margins_ref,
    amp_out,
    res_out,
    margins,
    edge,
    band,
    first,
    second,
    gathered_start,
    gathered_next,
    unfolded,
    ratio,
    sent,
    got,
    res_all,
    margin_sem,
    b_sem,
    gat_send,
    gat_fwd,
    gat_relay,
    gat_recv,
    fit_send,
    fit_recv,
    spread_send,
    res_recv,
    free_sem,
):
    me = lax.axis_index("pairs")
    z = lax.axis_index("fit")
    chips = n_pairs // 2
    chip, core = me // 2, lax.rem(me, 2)
    sibling = chip * 2 + (1 - core)
    pair_dev, width, _ = start_ref.shape
    per_pair = margins.shape[1]
    own_pairs = pair_dev // n_fit
    tail, fold, tail_rows = tail_shape(width)
    relayed = chips == 4
    near = (1, 2)
    early = gathered_next.shape == gathered_start.shape
    gathered = (gathered_start, gathered_next if early else gathered_start)
    bands = per_pair * tail // LANES
    per_band = LANES // tail

    def margin_copy(row):
        return pltpu.make_async_copy(
            margins_ref.at[row], margins.at[row], margin_sem.at[row]
        )

    copy_first = pltpu.make_async_copy(b_first_ref, first, b_sem.at[0])
    copy_second = pltpu.make_async_copy(b_second_ref, second, b_sem.at[1])
    copy_first.start()
    copy_second.start()
    for row in range(pair_dev):
        margin_copy(row).start()

    barrier = pltpu.get_barrier_semaphore()

    def same_core(step):
        return lax.rem(chip + step, chips) * 2 + core

    def at_chip(step):
        return flip(chip, step, chips) * 2 + core

    def fit_peer(step):
        return lax.rem(z + step, n_fit)

    def greet(sem):
        @pl.loop(1, chips)
        def _(step):
            pl.semaphore_signal(
                sem, inc=1, device_id={"pairs": same_core(step), "fit": z}
            )

        pl.semaphore_signal(sem, inc=1, device_id={"pairs": sibling, "fit": z})
        for step in range(1, n_fit):
            pl.semaphore_signal(
                sem, inc=1, device_id={"pairs": me, "fit": fit_peer(step)}
            )

    greeted = chips - 1 + 1 + n_fit - 1
    greet(barrier)

    def owner_at(turn):
        turn = lax.rem(turn, n_fit)
        half = turn // 2
        return jnp.where(lax.rem(turn, 2) == 0, half, n_fit - 1 - half)

    def row_at(turn):
        return owner_at(turn) * own_pairs + turn // n_fit

    def pack(ref, block):
        ref[pl.ds(0, width), :] = block[:, :LANES].astype(BF16)
        pieces = []
        for part in range(fold):
            low, high = part * tail_rows, min((part + 1) * tail_rows, width)
            piece = block[low:high, LANES:]
            if high - low < tail_rows:
                filler = jnp.zeros((tail_rows - (high - low), tail), block.dtype)
                piece = jnp.concatenate([piece, filler], axis=0)
            pieces.append(piece)
        ref[pl.ds(width, tail_rows), :] = jnp.concatenate(pieces, axis=1).astype(BF16)

    def unpack(ref):
        main = ref[pl.ds(0, width), :].astype(F32)
        lanes = ref[pl.ds(width, tail_rows), :].astype(F32)
        pieces = []
        for part in range(fold):
            rows = min(tail_rows, width - part * tail_rows)
            pieces.append(lanes[:rows, part * tail : (part + 1) * tail])
        return jnp.concatenate([main, jnp.concatenate(pieces, axis=0)], axis=1)

    rows_at = lax.broadcasted_iota(jnp.int32, (width, width), 0)
    cols_at = lax.broadcasted_iota(jnp.int32, (width, width), 1)

    def mask_of(row):
        count = count_ref[row]
        return (rows_at < count).astype(F32) * (cols_at < count).astype(F32)

    orbitals = lax.broadcasted_iota(jnp.int32, occ_ref.shape, 1)

    def occ_of(orbital):
        return jnp.sum(
            jnp.where(orbitals == orbital, occ_ref[...], 0.0), axis=1, keepdims=True
        )

    def denominator_of(row):
        across = jnp.broadcast_to(energy_ref[pl.ds(row, 1), :], (width, width))
        down = jnp.sum(
            jnp.where(rows_at == cols_at, across, 0.0), axis=1, keepdims=True
        )
        return down + across - (occ_of(list_ref[0, row]) + occ_of(list_ref[1, row]))

    @pl.loop(0, pair_dev)
    def _(row):
        pack(gathered[0].at[me * pair_dev + row], mask_of(row) * start_ref[row])

    pl.semaphore_wait(barrier, greeted)

    def turns(gather):
        return n_fit if gather == 0 else pair_dev

    def first_row(gather, turn):
        return owner_at(turn) * own_pairs if gather == 0 else row_at(turn)

    def gather_copy(gather, owner, row, send_sem, target):
        slot = owner * pair_dev + row
        if gather == 0:
            ref = gathered[0].at[pl.ds(slot, own_pairs)]
        else:
            ref = gathered[1].at[slot]
        return pltpu.make_async_remote_copy(
            src_ref=ref,
            dst_ref=ref,
            send_sem=send_sem,
            recv_sem=gat_recv.at[gather, slot],
            device_id=target,
        )

    def direct(gather, row, step, target):
        return gather_copy(
            gather,
            me,
            row,
            gat_send.at[gather, step, row],
            {"pairs": target, "fit": z},
        )

    def forward(gather, owner, row):
        return gather_copy(
            gather,
            owner,
            row,
            gat_fwd.at[gather, owner * pair_dev + row],
            {"pairs": sibling, "fit": z},
        )

    def relay(gather, owner, row, step):
        return gather_copy(
            gather,
            owner,
            row,
            gat_relay.at[gather, row],
            {"pairs": at_chip(step), "fit": z},
        )

    def spread(row, step):
        return gather_copy(
            1,
            me,
            row,
            spread_send.at[0, row, step],
            {"pairs": me, "fit": fit_peer(step)},
        )

    def arrived(gather, owner, row):
        forward(gather, owner, row).wait_recv()

    def send_plane(gather, row):
        if relayed:
            for step in near:
                direct(gather, row, step, at_chip(step)).start()
        else:

            @pl.loop(1, chips)
            def _(step):
                direct(gather, row, step, same_core(step)).start()

        forward(gather, me, row).start()

    def fill(gather, owner, row):
        slot = owner * pair_dev + row
        for index in range(own_pairs if gather == 0 else 1):
            lanes = gathered[gather][slot + index, pl.ds(width, tail_rows), :]
            for part in range(fold):
                rows = min(tail_rows, width - part * tail_rows)
                piece = lanes[:rows]
                if part:
                    at = part * tail
                    piece = jnp.concatenate([piece[:, at:], piece[:, :at]], axis=1)
                unfolded[slot + index, pl.ds(part * tail_rows, rows), :] = piece

    def take_near(gather, turn):
        row = first_row(gather, turn)
        if relayed:
            for step in near:
                owner = at_chip(step)
                arrived(gather, owner, row)
                forward(gather, owner, row).start()

                @pl.when(lax.rem(turn, 2) == step - 1)
                def _():
                    relay(gather, owner, row, 3 - step).start()

            for step in near:
                fill(gather, at_chip(step), row)
        else:

            @pl.loop(1, chips)
            def _(step):
                owner = same_core(chips - step)
                arrived(gather, owner, row)
                forward(gather, owner, row).start()
                fill(gather, owner, row)

        fill(gather, me, row)

    def take_far(gather, turn):
        if relayed:
            row = first_row(gather, turn)
            owner = at_chip(3)
            arrived(gather, owner, row)
            forward(gather, owner, row).start()
            fill(gather, owner, row)

    def take_sibling(gather, turn):
        row = first_row(gather, turn)

        @pl.loop(0, chips)
        def _(step):
            owner = lax.rem(chip + chips - step, chips) * 2 + (1 - core)
            arrived(gather, owner, row)
            fill(gather, owner, row)

    def finish_sends(gather):
        @pl.loop(0, turns(gather))
        def _(turn):
            row = first_row(gather, turn)
            if relayed:
                for step in near:
                    direct(gather, row, step, at_chip(step)).wait_send()
                relay(gather, me, row, 1).wait_send()

            @pl.loop(1, chips)
            def _(step):
                if not relayed:
                    direct(gather, row, step, same_core(step)).wait_send()
                forward(gather, same_core(step), row).wait_send()

            forward(gather, me, row).wait_send()

    def reduce_copy(iteration, turn, source, target):
        row = row_at(turn)
        return pltpu.make_async_remote_copy(
            src_ref=sent.at[iteration, row],
            dst_ref=got.at[iteration, turn // n_fit, source],
            send_sem=fit_send.at[iteration, row],
            recv_sem=fit_recv.at[iteration, turn // n_fit, source],
            device_id={"pairs": me, "fit": target},
        )

    def res_copy(row, step):
        return pltpu.make_async_remote_copy(
            src_ref=res_all.at[row],
            dst_ref=res_all.at[row],
            send_sem=spread_send.at[1, row, step],
            recv_sem=res_recv.at[row],
            device_id={"pairs": me, "fit": fit_peer(step)},
        )

    def couple(gather, row):
        mains, ends = [], []
        for col in range(per_pair):
            partner = partner_ref[row, col]
            amplitudes = jnp.concatenate(
                [gathered[gather][partner, pl.ds(0, width), :], unfolded[partner]],
                axis=1,
            )
            margin = jnp.concatenate(
                [margins[row, col, :, pl.ds(0, LANES)], edge[row, col]], axis=1
            )
            product = lax.dot_general(
                amplitudes,
                margin,
                (((1,), (1,)), ((), ())),
                preferred_element_type=F32,
            )
            product = (product * fock_ref[row, col]).astype(BF16)
            mains.append(product[:LANES])
            ends.append(product[LANES:])
        wide = jnp.concatenate(
            [margins[row, col, :, pl.ds(0, LANES)] for col in range(per_pair)]
            + [band[row, part] for part in range(bands)],
            axis=1,
        )
        return jnp.dot(
            wide, jnp.concatenate(mains + ends, axis=0), preferred_element_type=F32
        )

    for turn in range(n_fit):
        send_plane(0, first_row(0, turn))

    copy_first.wait()
    copy_second.wait()

    @pl.loop(0, pair_dev)
    def _(row):
        amp_out[row] = lax.dot_general(
            first[row],
            second[row],
            (((1,), (1,)), ((), ())),
            preferred_element_type=F32,
        )
        ratio[row] = mask_of(row) / denominator_of(row)
        margin_copy(row).wait()
        blank = jnp.zeros((width, LANES - tail), BF16)

        @pl.loop(0, bands)
        def _(part):
            ends = []
            for index in range(per_band):
                col = part * per_band + index
                piece = margins[row, col][:, LANES:]
                edge[row, col] = jnp.concatenate([piece, blank], axis=1)
                ends.append(piece)
            band[row, part] = jnp.concatenate(ends, axis=1)

        if pair_dev >= 2 * n_fit:

            @pl.when(lax.rem(row, 2) == 1)
            def _():
                @pl.when(row // 2 < n_fit)
                def _():
                    take_near(0, row // 2)

    if pair_dev < 2 * n_fit:
        for turn in range(n_fit):
            take_near(0, turn)
    for turn in range(n_fit):
        take_far(0, turn)

    @pl.loop(0, n_fit)
    def _(turn):
        take_sibling(0, turn)

    def collect(iteration, turn, total):
        for step in range(1, n_fit):
            peer = fit_peer(step)
            reduce_copy(iteration, turn, peer, z).wait_recv()
            total = total + unpack(got.at[iteration, turn // n_fit, peer])
        return total

    def update(turn, ref):
        row = row_at(turn)
        total = collect(0, turn, res_out[row] - amp_out[row])
        pack(ref, total * ratio[row])

    def publish(turn):
        @pl.when(owner_at(turn) == z)
        def _():
            row = row_at(turn)
            slot = gathered[1].at[me * pair_dev + row]
            if early:
                update(turn, slot)
            else:
                slot[...] = sent[0, row]
            for step in range(1, n_fit):
                spread(row, step).start()
            send_plane(1, row)

    def pass_on(turn):
        @pl.when(owner_at(turn) != z)
        def _():
            row = row_at(turn)
            arrived(1, me, row)
            send_plane(1, row)

    @pl.loop(0, pair_dev)
    def _(turn):
        row = row_at(turn)
        coupling = couple(0, row)
        res_out[row] = coupling

        @pl.when(owner_at(turn) != z)
        def _():
            pack(sent.at[0, row], coupling - amp_out[row])
            reduce_copy(0, turn, z, owner_at(turn)).start()

        if early:

            @pl.when(turn >= REDUCE_LAG)
            def _():
                publish(turn - REDUCE_LAG)

            @pl.when(turn >= SPREAD_LAG)
            def _():
                pass_on(turn - SPREAD_LAG)

    finish_sends(0)
    if early:
        publish_lag, pass_lag = REDUCE_LAG, SPREAD_LAG
    else:

        @pl.loop(0, own_pairs)
        def _(index):
            row = z * own_pairs + index
            order = jnp.where(2 * z < n_fit, 2 * z, 2 * (n_fit - 1 - z) + 1)
            update(index * n_fit + order, sent.at[0, row])

        greet(free_sem)
        pl.semaphore_wait(free_sem, greeted)
        publish_lag, pass_lag = pair_dev, pair_dev + 2

    def when_in(turn, action):
        @pl.when(jnp.logical_and(turn >= 0, turn < pair_dev))
        def _():
            action(turn)

    near_lag = max(pass_lag + 2, pair_dev)

    @pl.loop(pair_dev, near_lag + pair_dev + 1)
    def _(turn):
        when_in(turn - publish_lag, publish)
        when_in(turn - pass_lag, pass_on)
        when_in(turn - near_lag, functools.partial(take_near, 1))
        when_in(turn - near_lag - 1, functools.partial(take_far, 1))

    @pl.loop(0, pair_dev)
    def _(turn):
        take_sibling(1, turn)

    def settle(turn):
        @pl.when(owner_at(turn) == z)
        def _():
            row = row_at(turn)
            total = collect(1, turn, res_out[row])
            pack(res_all.at[row], mask_of(row) * total)
            for step in range(1, n_fit):
                res_copy(row, step).start()

    def write_out(turn):
        row = row_at(turn)

        @pl.when(owner_at(turn) != z)
        def _():
            res_copy(row, 1).wait_recv()

        residual = unpack(res_all.at[row])
        amplitudes = unpack(gathered[1].at[me * pair_dev + row])
        res_out[row] = residual
        amp_out[row] = amplitudes - residual * ratio[row]

    @pl.loop(0, pair_dev)
    def _(turn):
        row = row_at(turn)
        change = res_out[row] - couple(1, row)
        res_out[row] = change

        @pl.when(owner_at(turn) != z)
        def _():
            pack(sent.at[1, row], change)
            reduce_copy(1, turn, z, owner_at(turn)).start()

        @pl.when(turn >= REDUCE_LAG)
        def _():
            settle(turn - REDUCE_LAG)

        @pl.when(turn >= SPREAD_LAG)
        def _():
            write_out(turn - SPREAD_LAG)

    @pl.loop(pair_dev, pair_dev + SPREAD_LAG)
    def _(turn):
        when_in(turn - REDUCE_LAG, settle)
        write_out(turn - SPREAD_LAG)

    finish_sends(1)

    @pl.loop(0, pair_dev)
    def _(turn):
        row = row_at(turn)

        @pl.when(owner_at(turn) == z)
        def _():
            for step in range(1, n_fit):
                spread(row, step).wait_send()
                res_copy(row, step).wait_send()

        @pl.when(owner_at(turn) != z)
        def _():
            for iteration in range(ITERS):
                reduce_copy(iteration, turn, z, owner_at(turn)).wait_send()


def shards(
    n_pairs,
    n_fit,
    b_first,
    b_second,
    start_amplitudes,
    margins,
    fock_terms,
    partners,
    pno_energy,
    occ_energy,
    pair_list,
    pno_count,
):
    pair_dev, width, _ = start_amplitudes.shape
    own_pairs = pair_dev // n_fit
    per_pair = margins.shape[1]
    tail, _, tail_rows = tail_shape(width)
    block = (width + tail_rows, LANES)
    slots = n_pairs * pair_dev
    steps = max(n_pairs // 2, 3)
    out = jax.ShapeDtypeStruct(start_amplitudes.shape, F32)
    vmem = pl.BlockSpec(memory_space=pltpu.VMEM)
    smem = pl.BlockSpec(memory_space=pltpu.SMEM)
    hbm = pl.BlockSpec(memory_space=pl.ANY)
    return pl.pallas_call(
        functools.partial(kernel, n_pairs, n_fit),
        out_shape=(out, out),
        in_specs=[vmem, vmem, smem, smem, vmem, smem, smem, hbm, hbm, hbm],
        out_specs=(vmem, vmem),
        scratch_shapes=[
            pltpu.VMEM(margins.shape, BF16),
            pltpu.VMEM((pair_dev, per_pair, width, LANES), BF16),
            pltpu.VMEM((pair_dev, per_pair * tail // LANES, width, LANES), BF16),
            pltpu.VMEM(b_first.shape, BF16),
            pltpu.VMEM(b_second.shape, BF16),
            pltpu.VMEM((slots,) + block, BF16),
            pltpu.VMEM((slots if n_pairs == 8 else 1,) + block, BF16),
            pltpu.VMEM((slots, width, LANES), BF16),
            pltpu.VMEM((pair_dev, width, width), F32),
            pltpu.VMEM((ITERS, pair_dev) + block, BF16),
            pltpu.VMEM((ITERS, own_pairs, n_fit) + block, BF16),
            pltpu.VMEM((pair_dev,) + block, BF16),
            pltpu.SemaphoreType.DMA((pair_dev,)),
            pltpu.SemaphoreType.DMA((2,)),
            pltpu.SemaphoreType.DMA((ITERS, steps, pair_dev)),
            pltpu.SemaphoreType.DMA((ITERS, slots)),
            pltpu.SemaphoreType.DMA((ITERS, pair_dev)),
            pltpu.SemaphoreType.DMA((ITERS, slots)),
            pltpu.SemaphoreType.DMA((ITERS, pair_dev)),
            pltpu.SemaphoreType.DMA((ITERS, own_pairs, n_fit)),
            pltpu.SemaphoreType.DMA((2, pair_dev, n_fit)),
            pltpu.SemaphoreType.DMA((pair_dev,)),
            pltpu.SemaphoreType.REGULAR,
        ],
        compiler_params=pltpu.CompilerParams(
            collective_id=0, has_side_effects=True, vmem_limit_bytes=65000 * 1024
        ),
    )(
        start_amplitudes,
        pno_energy,
        fock_terms,
        partners,
        occ_energy.reshape(1, -1),
        pair_list.T,
        pno_count,
        b_first,
        b_second,
        margins,
    )


def solution(mesh):
    return jax.shard_map(
        functools.partial(shards, mesh.shape["pairs"], mesh.shape["fit"]),
        mesh=mesh,
        in_specs=(
            P("pairs", None, "fit"),
            P("pairs", None, "fit"),
            P("pairs", None, None),
            P("pairs", "fit", None, None),
            P("pairs", "fit"),
            P("pairs", "fit"),
            P("pairs", None),
            P(),
            P("pairs", None),
            P("pairs"),
        ),
        out_specs=(P("pairs", None, None), P("pairs", None, None)),
        check_vma=False,
    )
```

```python
import functools
import jax
import jax.numpy as jnp
from jax import lax
from jax.experimental import pallas as pl
from jax.experimental.pallas import tpu as pltpu
from jax.sharding import PartitionSpec as P

ITERS = 2
LANES = 128
SUBLANES = 16
REDUCE_LAG = 4
AT_ONCE = (8, 4)
DIAGONAL = 2
BATCH = 8
BF16 = jnp.bfloat16
F32 = jnp.float32


def flip(value, bits, size):
    result, place = 0, 1
    while place < size:
        one = (value // place) % 2
        other = (bits // place) % 2
        result = result + place * ((one + other) % 2)
        place *= 2
    return result


def tail_shape(width):
    tail = width - LANES
    fold = LANES // tail
    rows = -(-width // (fold * SUBLANES)) * SUBLANES
    return tail, fold, rows


def kernel(
    n_pairs,
    n_fit,
    start_ref,
    energy_ref,
    fock_ref,
    partner_ref,
    occ_ref,
    list_ref,
    count_ref,
    b_first_ref,
    b_second_ref,
    margins_ref,
    amp_out,
    res_out,
    margins,
    edge,
    band,
    first,
    second,
    gathered_start,
    gathered_next,
    unfolded,
    ratio,
    sent,
    got,
    res_all,
    held_even,
    held_odd,
    margin_sem,
    b_sem,
    gat_send,
    gat_fwd,
    gat_relay,
    gat_recv,
    fit_send,
    fit_recv,
    spread_send,
    res_recv,
    free_sem,
):
    me = lax.axis_index("pairs")
    z = lax.axis_index("fit")
    chips = n_pairs // 2
    chip, core = me // 2, lax.rem(me, 2)
    sibling = chip * 2 + (1 - core)
    pair_dev, width, _ = start_ref.shape
    per_pair = margins.shape[1]
    own_pairs = pair_dev // n_fit
    tail, fold, tail_rows = tail_shape(width)
    relayed = chips == 4
    near = (1, 2)
    early = gathered_next.shape == gathered_start.shape
    gathered = (gathered_start, gathered_next if early else gathered_start)
    bands = per_pair * tail // LANES
    per_band = LANES // tail

    def margin_copy(row):
        return pltpu.make_async_copy(
            margins_ref.at[row], margins.at[row], margin_sem.at[row]
        )

    copy_first = pltpu.make_async_copy(b_first_ref, first, b_sem.at[0])
    copy_second = pltpu.make_async_copy(b_second_ref, second, b_sem.at[1])
    copy_first.start()
    copy_second.start()
    for row in range(pair_dev):
        margin_copy(row).start()

    barrier = pltpu.get_barrier_semaphore()

    def same_core(step):
        return lax.rem(chip + step, chips) * 2 + core

    def at_chip(step):
        return flip(chip, step, chips) * 2 + core

    def fit_peer(step):
        return lax.rem(z + step, n_fit)

    def greet(sem):
        @pl.loop(1, chips)
        def _(step):
            pl.semaphore_signal(
                sem, inc=1, device_id={"pairs": same_core(step), "fit": z}
            )

        pl.semaphore_signal(sem, inc=1, device_id={"pairs": sibling, "fit": z})
        for step in range(1, n_fit):
            pl.semaphore_signal(
                sem, inc=1, device_id={"pairs": me, "fit": fit_peer(step)}
            )

    greeted = chips - 1 + 1 + n_fit - 1
    greet(barrier)

    def owner_at(turn):
        turn = lax.rem(turn, n_fit)
        half = turn // 2
        return jnp.where(lax.rem(turn, 2) == 0, half, n_fit - 1 - half)

    def row_at(turn):
        return owner_at(turn) * own_pairs + turn // n_fit

    def pack(ref, block):
        ref[pl.ds(0, width), :] = block[:, :LANES].astype(BF16)
        pieces = []
        for part in range(fold):
            low, high = part * tail_rows, min((part + 1) * tail_rows, width)
            piece = block[low:high, LANES:]
            if high - low < tail_rows:
                filler = jnp.zeros((tail_rows - (high - low), tail), block.dtype)
                piece = jnp.concatenate([piece, filler], axis=0)
            pieces.append(piece)
        ref[pl.ds(width, tail_rows), :] = jnp.concatenate(pieces, axis=1).astype(BF16)

    def unpack(ref):
        main = ref[pl.ds(0, width), :].astype(F32)
        lanes = ref[pl.ds(width, tail_rows), :].astype(F32)
        pieces = []
        for part in range(fold):
            rows = min(tail_rows, width - part * tail_rows)
            pieces.append(lanes[:rows, part * tail : (part + 1) * tail])
        return jnp.concatenate([main, jnp.concatenate(pieces, axis=0)], axis=1)

    rows_at = lax.broadcasted_iota(jnp.int32, (width, width), 0)
    cols_at = lax.broadcasted_iota(jnp.int32, (width, width), 1)

    def mask_of(row):
        count = count_ref[row]
        return (rows_at < count).astype(F32) * (cols_at < count).astype(F32)

    orbitals = lax.broadcasted_iota(jnp.int32, occ_ref.shape, 1)

    def occ_of(orbital):
        return jnp.sum(
            jnp.where(orbitals == orbital, occ_ref[...], 0.0), axis=1, keepdims=True
        )

    def denominator_of(row):
        across = jnp.broadcast_to(energy_ref[pl.ds(row, 1), :], (width, width))
        down = jnp.sum(
            jnp.where(rows_at == cols_at, across, 0.0), axis=1, keepdims=True
        )
        return down + across - (occ_of(list_ref[0, row]) + occ_of(list_ref[1, row]))

    @pl.loop(0, pair_dev)
    def _(row):
        pack(gathered[0].at[me * pair_dev + row], mask_of(row) * start_ref[row])

    pl.semaphore_wait(barrier, greeted)

    def turns(gather):
        return n_fit if gather == 0 else pair_dev

    def first_row(gather, turn):
        return owner_at(turn) * own_pairs if gather == 0 else row_at(turn)

    def gather_copy(gather, owner, row, send_sem, target):
        slot = owner * pair_dev + row
        if gather == 0:
            ref = gathered[0].at[pl.ds(slot, own_pairs)]
        else:
            ref = gathered[1].at[slot]
        return pltpu.make_async_remote_copy(
            src_ref=ref,
            dst_ref=ref,
            send_sem=send_sem,
            recv_sem=gat_recv.at[gather, slot],
            device_id=target,
        )

    def direct(gather, row, step, target):
        return gather_copy(
            gather,
            me,
            row,
            gat_send.at[gather, step, row],
            {"pairs": target, "fit": z},
        )

    def forward(gather, owner, row):
        return gather_copy(
            gather,
            owner,
            row,
            gat_fwd.at[gather, owner * pair_dev + row],
            {"pairs": sibling, "fit": z},
        )

    def relay(gather, owner, row, step):
        return gather_copy(
            gather,
            owner,
            row,
            gat_relay.at[gather, row],
            {"pairs": at_chip(step), "fit": z},
        )

    def spread(row, target):
        return gather_copy(
            1,
            me,
            row,
            spread_send.at[0, row, target],
            {"pairs": me, "fit": target},
        )

    chained = n_fit == 4
    inner = {0: 1, n_fit - 1: n_fit - 2} if chained else {}

    def each_target(kind, turn, owned, action):
        owner = owner_at(turn)
        at_once = turn >= (pair_dev - AT_ONCE[kind] if chained else 0)
        for target in range(n_fit):
            if target in inner:
                beside = z == inner[target]
                if owned:
                    wanted = jnp.logical_or(beside, at_once)
                else:
                    wanted = jnp.logical_and(beside, owner != target)
                    wanted = jnp.logical_and(wanted, jnp.logical_not(at_once))
                wanted = jnp.logical_and(wanted, z != target)
            elif owned:
                wanted = z != target
            else:
                continue
            pl.when(wanted)(functools.partial(action, target))

    def arrived(gather, owner, row):
        forward(gather, owner, row).wait_recv()

    def crosses(gather, row):
        if gather == 0:
            return False
        part, index = row // own_pairs, lax.rem(row, own_pairs)
        order = jnp.where(2 * part < n_fit, 2 * part, 2 * (n_fit - 1 - part) + 1)
        turn = index * n_fit + order
        return jnp.logical_or(turn < n_fit, turn >= pair_dev - DIAGONAL)

    def send_plane(gather, row):
        if relayed:
            for step in near:
                direct(gather, row, step, at_chip(step)).start()

            @pl.when(crosses(gather, row))
            def _():
                direct(gather, row, 3, at_chip(3)).start()
        else:

            @pl.loop(1, chips)
            def _(step):
                direct(gather, row, step, same_core(step)).start()

        forward(gather, me, row).start()

    def fill(gather):
        @pl.loop(0, unfolded.shape[0] // BATCH)
        def _(batch):
            for index in range(BATCH):
                slot = batch * BATCH + index
                lanes = gathered[gather][slot, pl.ds(width, tail_rows), :]
                for part in range(fold):
                    rows = min(tail_rows, width - part * tail_rows)
                    piece = lanes[:rows]
                    if part:
                        at = part * tail
                        piece = jnp.concatenate([piece[:, at:], piece[:, :at]], axis=1)
                    unfolded[slot, pl.ds(part * tail_rows, rows), :] = piece

    def near_turn(gather, step, turn):
        if gather == 1:
            return turn
        half = (n_fit + 2 - step) // 2
        return jnp.where(
            turn < half, 2 * turn + step - 1, 2 * (turn - half) + 2 - step
        )

    def take_near(gather, place):
        turn = place
        row = first_row(gather, turn)
        if relayed:
            for step in near:
                turn = near_turn(gather, step, place)
                row = first_row(gather, turn)
                owner = at_chip(step)
                arrived(gather, owner, row)
                forward(gather, owner, row).start()

                @pl.when(
                    jnp.logical_and(
                        lax.rem(turn, 2) == step - 1,
                        jnp.logical_not(crosses(gather, row)),
                    )
                )
                def _():
                    relay(gather, owner, row, 3 - step).start()

        else:

            @pl.loop(1, chips)
            def _(step):
                owner = same_core(chips - step)
                arrived(gather, owner, row)
                forward(gather, owner, row).start()

    def take_far(gather, turn):
        if relayed:
            row = first_row(gather, turn)
            owner = at_chip(3)
            arrived(gather, owner, row)
            forward(gather, owner, row).start()

    def take_sibling(gather, turn):
        row = first_row(gather, turn)

        @pl.loop(0, chips)
        def _(step):
            owner = lax.rem(chip + chips - step, chips) * 2 + (1 - core)
            arrived(gather, owner, row)

    def finish_sends(gather):
        @pl.loop(0, turns(gather))
        def _(turn):
            row = first_row(gather, turn)
            if relayed:
                for step in near:
                    direct(gather, row, step, at_chip(step)).wait_send()
                relayed_on = jnp.logical_not(crosses(gather, row))

                @pl.when(relayed_on)
                def _():
                    relay(gather, me, row, 1).wait_send()

                @pl.when(jnp.logical_not(relayed_on))
                def _():
                    direct(gather, row, 3, at_chip(3)).wait_send()

            @pl.loop(1, chips)
            def _(step):
                if not relayed:
                    direct(gather, row, step, same_core(step)).wait_send()
                forward(gather, same_core(step), row).wait_send()

            forward(gather, me, row).wait_send()

    def reduce_copy(iteration, turn, source, target):
        row = row_at(turn)
        return pltpu.make_async_remote_copy(
            src_ref=sent.at[iteration, row],
            dst_ref=got.at[iteration, turn // n_fit, source],
            send_sem=fit_send.at[iteration, row],
            recv_sem=fit_recv.at[iteration, turn // n_fit, source],
            device_id={"pairs": me, "fit": target},
        )

    def res_copy(row, target):
        return pltpu.make_async_remote_copy(
            src_ref=res_all.at[row],
            dst_ref=res_all.at[row],
            send_sem=spread_send.at[1, row, target],
            recv_sem=res_recv.at[row],
            device_id={"pairs": me, "fit": target},
        )

    ends_at = per_pair * LANES

    def inner_products(gather, row, held):
        for col in range(per_pair):
            partner = partner_ref[row, col]
            amplitudes = jnp.concatenate(
                [gathered[gather][partner, pl.ds(0, width), :], unfolded[partner]],
                axis=1,
            )
            margin = jnp.concatenate(
                [margins[row, col, :, pl.ds(0, LANES)], edge[row, col]], axis=1
            )
            product = lax.dot_general(
                amplitudes,
                margin,
                (((1,), (1,)), ((), ())),
                preferred_element_type=F32,
            )
            product = (product * fock_ref[row, col]).astype(BF16)
            held[pl.ds(col * LANES, LANES), :] = product[:LANES]
            held[pl.ds(ends_at + col * tail, tail), :] = product[LANES:]

    def outer_products(row, held):
        wide = jnp.concatenate(
            [margins[row, col, :, pl.ds(0, LANES)] for col in range(per_pair)]
            + [band[row, part] for part in range(bands)],
            axis=1,
        )
        return jnp.dot(wide, held[...], preferred_element_type=F32)

    def couple_all(gather, action):
        inner_products(gather, row_at(0), held_even)

        def two_rows(turn, more):
            coupling = outer_products(row_at(turn), held_even)
            inner_products(gather, row_at(turn + 1), held_odd)
            action(turn, coupling)
            coupling = outer_products(row_at(turn + 1), held_odd)
            if more:
                inner_products(gather, row_at(turn + 2), held_even)
            action(turn + 1, coupling)

        @pl.loop(0, pair_dev // 2 - 1)
        def _(step):
            two_rows(2 * step, True)

        two_rows(pair_dev - 2, False)

    for place in range(n_fit):
        if relayed:
            for step in near:
                row = first_row(0, near_turn(0, step, place))
                direct(0, row, step, at_chip(step)).start()
            forward(0, me, first_row(0, place)).start()
        else:
            send_plane(0, first_row(0, place))

    copy_first.wait()
    copy_second.wait()

    @pl.loop(0, pair_dev)
    def _(row):
        amp_out[row] = lax.dot_general(
            first[row],
            second[row],
            (((1,), (1,)), ((), ())),
            preferred_element_type=F32,
        )
        ratio[row] = mask_of(row) / denominator_of(row)
        margin_copy(row).wait()
        blank = jnp.zeros((width, LANES - tail), BF16)

        @pl.loop(0, bands)
        def _(part):
            ends = []
            for index in range(per_band):
                col = part * per_band + index
                piece = margins[row, col][:, LANES:]
                edge[row, col] = jnp.concatenate([piece, blank], axis=1)
                ends.append(piece)
            band[row, part] = jnp.concatenate(ends, axis=1)

        if pair_dev >= 2 * n_fit:

            @pl.when(lax.rem(row, 2) == 1)
            def _():
                @pl.when(row // 2 < n_fit)
                def _():
                    take_near(0, row // 2)

    if pair_dev < 2 * n_fit:
        for turn in range(n_fit):
            take_near(0, turn)
    for turn in range(n_fit):
        take_far(0, turn)

    @pl.loop(0, n_fit)
    def _(turn):
        take_sibling(0, turn)

    fill(0)

    def collect(iteration, turn, total):
        for step in range(1, n_fit):
            peer = fit_peer(step)
            reduce_copy(iteration, turn, peer, z).wait_recv()
            total = total + unpack(got.at[iteration, turn // n_fit, peer])
        return total

    def when_in(turn, action):
        @pl.when(jnp.logical_and(turn >= 0, turn < pair_dev))
        def _():
            action(turn)

    def update(turn, ref):
        row = row_at(turn)
        total = collect(0, turn, res_out[row] - amp_out[row])
        pack(ref, total * ratio[row])

    def publish(turn):
        @pl.when(owner_at(turn) == z)
        def _():
            row = row_at(turn)
            slot = gathered[1].at[me * pair_dev + row]
            if early:
                update(turn, slot)
            else:
                slot[...] = sent[0, row]
            each_target(0, turn, True, lambda target: spread(row, target).start())
            send_plane(1, row)

    def pass_on(turn):
        @pl.when(owner_at(turn) != z)
        def _():
            row = row_at(turn)
            arrived(1, me, row)
            each_target(0, turn, False, lambda target: spread(row, target).start())
            send_plane(1, row)

    def after_first(turn, coupling):
        row = row_at(turn)
        res_out[row] = coupling

        @pl.when(owner_at(turn) != z)
        def _():
            pack(sent.at[0, row], coupling - amp_out[row])
            reduce_copy(0, turn, z, owner_at(turn)).start()

        if early:
            when_in(turn - REDUCE_LAG, publish)

    couple_all(0, after_first)

    if early:

        @pl.loop(pair_dev - REDUCE_LAG, pair_dev - 2)
        def _(turn):
            publish(turn)

        finish_sends(0)
    else:
        finish_sends(0)

        @pl.loop(0, own_pairs)
        def _(index):
            row = z * own_pairs + index
            order = jnp.where(2 * z < n_fit, 2 * z, 2 * (n_fit - 1 - z) + 1)
            update(index * n_fit + order, sent.at[0, row])

        greet(free_sem)
        pl.semaphore_wait(free_sem, greeted)

        @pl.loop(0, pair_dev)
        def _(turn):
            publish(turn)

    @pl.loop(0, pair_dev + 4)
    def _(turn):
        when_in(turn, pass_on)
        if early:
            when_in(turn + pair_dev - 2, publish)
        when_in(turn - 3, functools.partial(take_near, 1))
        when_in(turn - 4, functools.partial(take_far, 1))

    @pl.loop(0, pair_dev)
    def _(turn):
        take_sibling(1, turn)

    fill(1)

    def settle(turn):
        @pl.when(owner_at(turn) == z)
        def _():
            row = row_at(turn)
            total = collect(1, turn, res_out[row])
            pack(res_all.at[row], mask_of(row) * total)
            each_target(1, turn, True, lambda target: res_copy(row, target).start())

    def pass_res(turn):
        @pl.when(owner_at(turn) != z)
        def _():
            row = row_at(turn)
            res_copy(row, 0).wait_recv()
            each_target(1, turn, False, lambda target: res_copy(row, target).start())

    def write_out(turn):
        row = row_at(turn)

        residual = unpack(res_all.at[row])
        amplitudes = unpack(gathered[1].at[me * pair_dev + row])
        res_out[row] = residual
        amp_out[row] = amplitudes - residual * ratio[row]

    def after_second(turn, coupling):
        row = row_at(turn)
        change = res_out[row] - coupling
        res_out[row] = change

        @pl.when(owner_at(turn) != z)
        def _():
            pack(sent.at[1, row], change)
            reduce_copy(1, turn, z, owner_at(turn)).start()

        when_in(turn - REDUCE_LAG, settle)

    couple_all(1, after_second)

    @pl.loop(pair_dev - REDUCE_LAG, pair_dev - 2)
    def _(turn):
        settle(turn)

    @pl.loop(0, pair_dev + 2)
    def _(turn):
        when_in(turn, pass_res)
        when_in(turn + pair_dev - 2, settle)
        when_in(turn - 2, write_out)

    finish_sends(1)

    @pl.loop(0, pair_dev)
    def _(turn):
        row = row_at(turn)

        def wait_spread(target):
            spread(row, target).wait_send()

        def wait_res(target):
            res_copy(row, target).wait_send()

        @pl.when(owner_at(turn) == z)
        def _():
            each_target(0, turn, True, wait_spread)
            each_target(1, turn, True, wait_res)

        @pl.when(owner_at(turn) != z)
        def _():
            each_target(0, turn, False, wait_spread)
            each_target(1, turn, False, wait_res)
            for iteration in range(ITERS):
                reduce_copy(iteration, turn, z, owner_at(turn)).wait_send()


def shards(
    n_pairs,
    n_fit,
    b_first,
    b_second,
    start_amplitudes,
    margins,
    fock_terms,
    partners,
    pno_energy,
    occ_energy,
    pair_list,
    pno_count,
):
    pair_dev, width, _ = start_amplitudes.shape
    own_pairs = pair_dev // n_fit
    per_pair = margins.shape[1]
    tail, _, tail_rows = tail_shape(width)
    block = (width + tail_rows, LANES)
    slots = n_pairs * pair_dev
    steps = max(n_pairs // 2, 3)
    out = jax.ShapeDtypeStruct(start_amplitudes.shape, F32)
    vmem = pl.BlockSpec(memory_space=pltpu.VMEM)
    smem = pl.BlockSpec(memory_space=pltpu.SMEM)
    hbm = pl.BlockSpec(memory_space=pl.ANY)
    return pl.pallas_call(
        functools.partial(kernel, n_pairs, n_fit),
        out_shape=(out, out),
        in_specs=[vmem, vmem, smem, smem, vmem, smem, smem, hbm, hbm, hbm],
        out_specs=(vmem, vmem),
        scratch_shapes=[
            pltpu.VMEM(margins.shape, BF16),
            pltpu.VMEM((pair_dev, per_pair, width, LANES), BF16),
            pltpu.VMEM((pair_dev, per_pair * tail // LANES, width, LANES), BF16),
            pltpu.VMEM(b_first.shape, BF16),
            pltpu.VMEM(b_second.shape, BF16),
            pltpu.VMEM((slots,) + block, BF16),
            pltpu.VMEM((slots if n_pairs == 8 else 1,) + block, BF16),
            pltpu.VMEM((slots, width, LANES), BF16),
            pltpu.VMEM((pair_dev, width, width), F32),
            pltpu.VMEM((ITERS, pair_dev) + block, BF16),
            pltpu.VMEM((ITERS, own_pairs, n_fit) + block, BF16),
            pltpu.VMEM((pair_dev,) + block, BF16),
            pltpu.VMEM((per_pair * width, width), BF16),
            pltpu.VMEM((per_pair * width, width), BF16),
            pltpu.SemaphoreType.DMA((pair_dev,)),
            pltpu.SemaphoreType.DMA((2,)),
            pltpu.SemaphoreType.DMA((ITERS, steps, pair_dev)),
            pltpu.SemaphoreType.DMA((ITERS, slots)),
            pltpu.SemaphoreType.DMA((ITERS, pair_dev)),
            pltpu.SemaphoreType.DMA((ITERS, slots)),
            pltpu.SemaphoreType.DMA((ITERS, pair_dev)),
            pltpu.SemaphoreType.DMA((ITERS, own_pairs, n_fit)),
            pltpu.SemaphoreType.DMA((2, pair_dev, n_fit)),
            pltpu.SemaphoreType.DMA((pair_dev,)),
            pltpu.SemaphoreType.REGULAR,
        ],
        compiler_params=pltpu.CompilerParams(
            collective_id=0, has_side_effects=True, vmem_limit_bytes=65000 * 1024
        ),
    )(
        start_amplitudes,
        pno_energy,
        fock_terms,
        partners,
        occ_energy.reshape(1, -1),
        pair_list.T,
        pno_count,
        b_first,
        b_second,
        margins,
    )


def solution(mesh):
    return jax.shard_map(
        functools.partial(shards, mesh.shape["pairs"], mesh.shape["fit"]),
        mesh=mesh,
        in_specs=(
            P("pairs", None, "fit"),
            P("pairs", None, "fit"),
            P("pairs", None, None),
            P("pairs", "fit", None, None),
            P("pairs", "fit"),
            P("pairs", "fit"),
            P("pairs", None),
            P(),
            P("pairs", None),
            P("pairs"),
        ),
        out_specs=(P("pairs", None, None), P("pairs", None, None)),
        check_vma=False,
    )
```

```python
import functools
import jax
import jax.numpy as jnp
from jax import lax
from jax.experimental import pallas as pl
from jax.experimental.pallas import tpu as pltpu
from jax.sharding import PartitionSpec as P

ITERS = 2
LANES = 128
SUBLANES = 16
BATCH = 8
BF16 = jnp.bfloat16
F32 = jnp.float32


def flip(value, bits, size):
    result, place = 0, 1
    while place < size:
        one = (value // place) % 2
        other = (bits // place) % 2
        result = result + place * ((one + other) % 2)
        place *= 2
    return result


def tail_shape(width):
    tail = width - LANES
    fold = LANES // tail
    rows = -(-width // (fold * SUBLANES)) * SUBLANES
    return tail, fold, rows


class Parts:
    def __init__(self, ref, size):
        self.ref, self.size, self.at = ref, size, self

    def __getitem__(self, slot):
        return self.ref.at[pl.ds(slot * self.size, self.size)]


def kernel(
    n_pairs,
    n_fit,
    start_ref,
    energy_ref,
    fock_ref,
    partner_ref,
    occ_ref,
    list_ref,
    count_ref,
    b_first_ref,
    b_second_ref,
    margins_ref,
    amp_out,
    res_out,
    margins,
    edge,
    band,
    b_hold,
    gathered_pairs,
    unfolded,
    amp_own,
    ratio,
    coup_send,
    coup_recv,
    res_all,
    margin_sem,
    b_sem,
    gat_send,
    gat_fwd,
    gat_relay,
    gat_recv,
    fit_send,
    fit_recv,
    free_sem,
):
    int_own, coup_own = amp_out, res_out
    me = lax.axis_index("pairs")
    z = lax.axis_index("fit")
    chips = n_pairs // 2
    chip, core = me // 2, lax.rem(me, 2)
    sibling = chip * 2 + (1 - core)
    pair_dev, width, _ = start_ref.shape
    per_pair = margins.shape[1]
    own_pairs = pair_dev // n_fit
    tail, fold, tail_rows = tail_shape(width)
    bands = per_pair * tail // LANES
    per_band = LANES // tail
    gathered = Parts(gathered_pairs, own_pairs)

    def margin_copy(row):
        return pltpu.make_async_copy(
            margins_ref.at[row], margins.at[row], margin_sem.at[row]
        )

    tiles = b_first_ref.shape[2] // LANES
    held = unfolded if b_hold.shape[0] == 1 else b_hold

    def b_copy(which, tile):
        return pltpu.make_async_copy(
            (b_first_ref, b_second_ref)[which].at[:, :, pl.ds(tile * LANES, LANES)],
            held.at[pl.ds((which * tiles + tile) * pair_dev, pair_dev)],
            b_sem.at[which, tile],
        )

    for tile in range(tiles):
        b_copy(0, tile).start()
        b_copy(1, tile).start()
    for row in range(pair_dev):
        margin_copy(row).start()

    barrier = pltpu.get_barrier_semaphore()

    def same_core(step):
        return lax.rem(chip + step, chips) * 2 + core

    def part_at(step):
        if n_fit & (n_fit - 1):
            return lax.rem(2 * n_fit - z - step, n_fit)
        return flip(z, step, n_fit)

    def greet(sem):
        @pl.loop(1, chips)
        def _(step):
            pl.semaphore_signal(
                sem, inc=1, device_id={"pairs": same_core(step), "fit": z}
            )

        pl.semaphore_signal(sem, inc=1, device_id={"pairs": sibling, "fit": z})
        for step in range(1, n_fit):
            pl.semaphore_signal(
                sem,
                inc=1,
                device_id={"pairs": me, "fit": part_at(step)},
            )

    greeted = chips - 1 + 1 + n_fit - 1
    greet(barrier)

    def pack_block(ref, block):
        ref[pl.ds(0, width), :] = block[:, :LANES].astype(BF16)
        pieces = []
        for part in range(fold):
            low, high = part * tail_rows, min((part + 1) * tail_rows, width)
            piece = block[low:high, LANES:]
            if high - low < tail_rows:
                filler = jnp.zeros((tail_rows - (high - low), tail), block.dtype)
                piece = jnp.concatenate([piece, filler], axis=0)
            pieces.append(piece)
        ref[pl.ds(width, tail_rows), :] = jnp.concatenate(pieces, axis=1).astype(BF16)

    def unpack_block(ref):
        main = ref[pl.ds(0, width), :].astype(F32)
        lanes = ref[pl.ds(width, tail_rows), :].astype(F32)
        pieces = []
        for part in range(fold):
            rows = min(tail_rows, width - part * tail_rows)
            pieces.append(lanes[:rows, part * tail : (part + 1) * tail])
        return jnp.concatenate([main, jnp.concatenate(pieces, axis=0)], axis=1)

    def pack(ref, blocks):
        for index, block in enumerate(blocks):
            pack_block(ref.at[index], block)

    def unpack(ref, index):
        return unpack_block(ref.at[index])

    rows_at = lax.broadcasted_iota(jnp.int32, (width, width), 0)
    cols_at = lax.broadcasted_iota(jnp.int32, (width, width), 1)

    def mask_of(row):
        count = count_ref[row]
        keep = (rows_at < count).astype(F32) * (cols_at < count).astype(F32)
        return keep

    orbitals = lax.broadcasted_iota(jnp.int32, occ_ref.shape, 1)

    def occ_of(orbital):
        return jnp.sum(
            jnp.where(orbitals == orbital, occ_ref[...], 0.0), axis=1, keepdims=True
        )

    def denominator_of(row):
        across = jnp.broadcast_to(energy_ref[pl.ds(row, 1), :], (width, width))
        down = jnp.sum(
            jnp.where(rows_at == cols_at, across, 0.0), axis=1, keepdims=True
        )
        return down + across - (occ_of(list_ref[0, row]) + occ_of(list_ref[1, row]))

    @pl.loop(0, n_fit)
    def _(part):
        pack(
            gathered.at[me * n_fit + part],
            [
                mask_of(part * own_pairs + index) * start_ref[part * own_pairs + index]
                for index in range(own_pairs)
            ],
        )

    pl.semaphore_wait(barrier, greeted)

    def direct(owner, part, step, target):
        slot = owner * n_fit + part
        return pltpu.make_async_remote_copy(
            src_ref=gathered.at[slot],
            dst_ref=gathered.at[slot],
            send_sem=gat_send.at[step, part],
            recv_sem=gat_recv.at[slot],
            device_id={"pairs": target, "fit": z},
        )

    def forward(owner, part):
        slot = owner * n_fit + part
        return pltpu.make_async_remote_copy(
            src_ref=gathered.at[slot],
            dst_ref=gathered.at[slot],
            send_sem=gat_fwd.at[slot],
            recv_sem=gat_recv.at[slot],
            device_id={"pairs": sibling, "fit": z},
        )

    relayed = chips == 4
    near = (1, 2) if relayed else ()

    def at_chip(step):
        return flip(chip, step, chips) * 2 + core

    def relay(owner, part, step):
        slot = owner * n_fit + part
        return pltpu.make_async_remote_copy(
            src_ref=gathered.at[slot],
            dst_ref=gathered.at[slot],
            send_sem=gat_relay.at[slot],
            recv_sem=gat_recv.at[slot],
            device_id={"pairs": at_chip(step), "fit": z},
        )

    def send_part(part):
        if relayed:
            for step in near:
                direct(me, part, step, at_chip(step)).start()
        else:

            @pl.loop(1, chips)
            def _(step):
                direct(me, part, step, same_core(step)).start()

        forward(me, part).start()

    def fill():
        @pl.loop(0, unfolded.shape[0] // BATCH)
        def _(batch):
            for index in range(BATCH):
                slot = batch * BATCH + index
                lanes = gathered_pairs[slot, pl.ds(width, tail_rows), :]
                for part in range(fold):
                    rows = min(tail_rows, width - part * tail_rows)
                    piece = lanes[:rows]
                    if part:
                        at = part * tail
                        piece = jnp.concatenate([piece[:, at:], piece[:, :at]], axis=1)
                    unfolded[slot, pl.ds(part * tail_rows, rows), :] = piece

    def take_direct(turn):
        part = part_at(turn)
        if relayed:
            for step in near:
                owner = at_chip(step)
                direct(owner, part, step, me).wait_recv()
                if step - 1 == turn % 2:
                    relay(owner, part, 3 - step).start()
                forward(owner, part).start()
        else:

            @pl.loop(1, chips)
            def _(step):
                owner = same_core(chips - step)
                direct(owner, part, step, me).wait_recv()
                forward(owner, part).start()

    def take_far(turn):
        part = part_at(turn)
        if relayed:
            owner = at_chip(3)
            direct(owner, part, 1, me).wait_recv()
            forward(owner, part).start()

    def take_sibling():
        @pl.loop(0, n_fit)
        def _(turn):
            part = part_at(turn)

            @pl.loop(0, chips)
            def _(step):
                owner = lax.rem(chip + chips - step, chips) * 2 + (1 - core)
                forward(owner, part).wait_recv()

        fill()

    def finish_sends():
        if relayed:
            for turn in range(n_fit):
                part = part_at(turn)
                for step in near:
                    direct(me, part, step, at_chip(step)).wait_send()
                    if step - 1 == turn % 2:
                        relay(at_chip(step), part, 3 - step).wait_send()

        @pl.loop(0, n_fit)
        def _(part):
            @pl.loop(1, chips)
            def _(step):
                if not relayed:
                    direct(me, part, step, same_core(step)).wait_send()
                forward(same_core(step), part).wait_send()

            forward(me, part).wait_send()

    def fit_copy(kind, step, index, source, target_ref):
        return pltpu.make_async_remote_copy(
            src_ref=source,
            dst_ref=target_ref,
            send_sem=fit_send.at[kind, step, index],
            recv_sem=fit_recv.at[kind, step, index],
            device_id={"pairs": me, "fit": part_at(step)},
        )

    def scatter_copy(iteration, step, index):
        return fit_copy(
            iteration,
            step,
            index,
            coup_send.at[iteration, step, index],
            coup_recv.at[iteration, step, index],
        )

    def high_copy(step, slot):
        return fit_copy(HIGH, step, 0, gathered.at[slot], gathered.at[slot])

    def res_copy(step, part, index):
        ref = res_all.at[part, index]
        return fit_copy(RES, step, index, ref, ref)

    def couple(iteration, row):
        mains, ends = [], []
        for col in range(per_pair):
            partner = partner_ref[row, col]
            amplitudes = jnp.concatenate(
                [gathered_pairs[partner, pl.ds(0, width), :], unfolded[partner]],
                axis=1,
            )
            margin = jnp.concatenate(
                [margins[row, col, :, pl.ds(0, LANES)], edge[row, col]], axis=1
            )
            product = lax.dot_general(
                amplitudes,
                margin,
                (((1,), (1,)), ((), ())),
                preferred_element_type=F32,
            )
            product = (product * fock_ref[row, col]).astype(BF16)
            mains.append(product[:LANES])
            ends.append(product[LANES:])
        wide = jnp.concatenate(
            [margins[row, col, :, pl.ds(0, LANES)] for col in range(per_pair)]
            + [band[row, part] for part in range(bands)],
            axis=1,
        )
        coupling = jnp.dot(
            wide, jnp.concatenate(mains + ends, axis=0), preferred_element_type=F32
        )
        coup_own[row] = coup_own[row] - coupling if iteration else coupling

    HIGH, RES = ITERS, ITERS + 1

    def partial_of(iteration, row):
        return coup_own[row] if iteration else coup_own[row] - int_own[row]


    @pl.loop(0, n_fit)
    def _(part):
        send_part(part_at(part))

    for tile in range(tiles):
        b_copy(0, tile).wait()
        b_copy(1, tile).wait()

    def b_row(which, row):
        return jnp.concatenate(
            [held[(which * tiles + tile) * pair_dev + row] for tile in range(tiles)],
            axis=1,
        )

    def integrals_of(row):
        return lax.dot_general(
            b_row(0, row),
            b_row(1, row),
            (((1,), (1,)), ((), ())),
            preferred_element_type=F32,
        )

    def prepare(row):
        int_own[row] = integrals_of(row)
        ratio[row] = mask_of(row) / denominator_of(row)
        margin_copy(row).wait()
        blank = jnp.zeros((width, LANES - tail), BF16)

        @pl.loop(0, bands)
        def _(part):
            pieces = []
            for index in range(per_band):
                col = part * per_band + index
                piece = margins[row, col][:, LANES:]
                edge[row, col] = jnp.concatenate([piece, blank], axis=1)
                pieces.append(piece)
            band[row, part] = jnp.concatenate(pieces, axis=1)

    for turn in range(n_fit):

        @pl.loop(turn * own_pairs, (turn + 1) * own_pairs)
        def _(row):
            prepare(row)

        take_direct(turn)
    for turn in range(n_fit):
        take_far(turn)
    take_sibling()

    def finish(iteration, index):
        row = z * own_pairs + index
        total = partial_of(iteration, row)
        for turn in range(1, n_fit):
            step = n_fit - turn
            scatter_copy(iteration, step, index).wait()
            total = total + unpack_block(coup_recv.at[iteration, step, index])
        if iteration == 0:
            amp_own[index] = total * ratio[row]
        else:
            pack_block(res_all.at[z, index], mask_of(row) * total)
            for step in range(1, n_fit):
                res_copy(step, z, index).start()

    for iteration in range(ITERS):

        @pl.loop(0, pair_dev)
        def _(turn):
            index = turn // n_fit
            step = n_fit - 1 - lax.rem(turn, n_fit)
            row = part_at(step) * own_pairs + index
            couple(iteration, row)

            @pl.when(step > 0)
            def _():
                pack_block(
                    coup_send.at[iteration, step, index], partial_of(iteration, row)
                )
                scatter_copy(iteration, step, index).start()

        if iteration < ITERS - 1:
            finish_sends()
            greet(free_sem)
            for index in range(own_pairs):
                finish(iteration, index)
            pl.semaphore_wait(free_sem, greeted)
            mine = me * n_fit + z
            pack(gathered.at[mine], [amp_own[index] for index in range(own_pairs)])
            for step in range(1, n_fit):
                high_copy(step, mine).start()
            send_part(z)
            for turn in range(1, n_fit):
                part = part_at(turn)
                high_copy(turn, me * n_fit + part).wait_recv()
                send_part(part)
                take_direct(turn - 1)
                if turn > 1:
                    take_far(turn - 2)
            take_direct(n_fit - 1)
            for turn in range(max(n_fit - 2, 0), n_fit):
                take_far(turn)
            take_sibling()
            for step in range(1, n_fit):
                high_copy(step, mine).wait_send()
        else:
            for index in range(own_pairs):
                finish(iteration, index)

    finish_sends()

    @pl.loop(0, pair_dev)
    def _(turn):
        index, step = turn // n_fit, lax.rem(turn, n_fit)
        part = part_at(step)

        @pl.when(step > 0)
        def _():
            res_copy(step, part, index).wait_recv()

        row = part * own_pairs + index
        residual = unpack_block(res_all.at[part, index])
        amplitudes = unpack(gathered.at[me * n_fit + part], index)
        res_out[row] = residual
        amp_out[row] = amplitudes - residual * ratio[row]

    for index in range(own_pairs):
        for step in range(1, n_fit):
            res_copy(step, z, index).wait_send()


def shards(
    n_pairs,
    n_fit,
    b_first,
    b_second,
    start_amplitudes,
    margins,
    fock_terms,
    partners,
    pno_energy,
    occ_energy,
    pair_list,
    pno_count,
):
    pair_dev, width, _ = start_amplitudes.shape
    own_pairs = pair_dev // n_fit
    per_pair = margins.shape[1]
    tail, _, tail_rows = tail_shape(width)
    block = (width + tail_rows, LANES)
    packed = (own_pairs,) + block
    slots = n_pairs * n_fit
    b_slots = 2 * pair_dev * b_first.shape[2] // LANES
    if b_slots <= n_pairs * pair_dev:
        b_slots = 1
    out = jax.ShapeDtypeStruct(start_amplitudes.shape, F32)
    vmem = pl.BlockSpec(memory_space=pltpu.VMEM)
    smem = pl.BlockSpec(memory_space=pltpu.SMEM)
    hbm = pl.BlockSpec(memory_space=pl.ANY)
    return pl.pallas_call(
        functools.partial(kernel, n_pairs, n_fit),
        out_shape=(out, out),
        in_specs=[vmem, vmem, smem, smem, vmem, smem, smem, hbm, hbm, hbm],
        out_specs=(vmem, vmem),
        scratch_shapes=[
            pltpu.VMEM(margins.shape, BF16),
            pltpu.VMEM((pair_dev, per_pair, width, LANES), BF16),
            pltpu.VMEM((pair_dev, per_pair * tail // LANES, width, LANES), BF16),
            pltpu.VMEM((b_slots, width, LANES), BF16),
            pltpu.VMEM((n_pairs * pair_dev,) + block, BF16),
            pltpu.VMEM((n_pairs * pair_dev, width, LANES), BF16),
            pltpu.VMEM((own_pairs, width, width), F32),
            pltpu.VMEM((pair_dev, width, width), F32),
            pltpu.VMEM((ITERS, n_fit) + packed, BF16),
            pltpu.VMEM((ITERS, n_fit) + packed, BF16),
            pltpu.VMEM((n_fit,) + packed, BF16),
            pltpu.SemaphoreType.DMA((pair_dev,)),
            pltpu.SemaphoreType.DMA((2, b_first.shape[2] // LANES)),
            pltpu.SemaphoreType.DMA((n_pairs // 2, n_fit)),
            pltpu.SemaphoreType.DMA((slots,)),
            pltpu.SemaphoreType.DMA((slots,)),
            pltpu.SemaphoreType.DMA((slots,)),
            pltpu.SemaphoreType.DMA((ITERS + 2, n_fit, own_pairs)),
            pltpu.SemaphoreType.DMA((ITERS + 2, n_fit, own_pairs)),
            pltpu.SemaphoreType.REGULAR,
        ],
        compiler_params=pltpu.CompilerParams(
            collective_id=0, has_side_effects=True, vmem_limit_bytes=65000 * 1024
        ),
    )(
        start_amplitudes,
        pno_energy,
        fock_terms,
        partners,
        occ_energy.reshape(1, -1),
        pair_list.T,
        pno_count,
        b_first,
        b_second,
        margins,
    )


def solution(mesh):
    return jax.shard_map(
        functools.partial(shards, mesh.shape["pairs"], mesh.shape["fit"]),
        mesh=mesh,
        in_specs=(
            P("pairs", None, "fit"),
            P("pairs", None, "fit"),
            P("pairs", None, None),
            P("pairs", "fit", None, None),
            P("pairs", "fit"),
            P("pairs", "fit"),
            P("pairs", None),
            P(),
            P("pairs", None),
            P("pairs"),
        ),
        out_specs=(P("pairs", None, None), P("pairs", None, None)),
        check_vma=False,
    )
```

```python
import functools
import jax
import jax.numpy as jnp
from jax import lax
from jax.experimental import pallas as pl
from jax.experimental.pallas import tpu as pltpu
from jax.sharding import PartitionSpec as P

ITERS = 2
LANES = 128
SUBLANES = 16
BATCH = 8
BF16 = jnp.bfloat16
F32 = jnp.float32


def flip(value, bits, size):
    result, place = 0, 1
    while place < size:
        one = (value // place) % 2
        other = (bits // place) % 2
        result = result + place * ((one + other) % 2)
        place *= 2
    return result


def tail_shape(width):
    tail = width - LANES
    fold = LANES // tail
    rows = -(-width // (fold * SUBLANES)) * SUBLANES
    return tail, fold, rows


class Parts:
    def __init__(self, ref, size):
        self.ref, self.size, self.at = ref, size, self

    def __getitem__(self, slot):
        return self.ref.at[pl.ds(slot * self.size, self.size)]


def kernel(
    n_pairs,
    n_fit,
    start_ref,
    energy_ref,
    fock_ref,
    partner_ref,
    occ_ref,
    list_ref,
    count_ref,
    b_first_ref,
    b_second_ref,
    margins_ref,
    amp_out,
    res_out,
    margins,
    edge,
    band,
    b_hold,
    gathered_pairs,
    unfolded,
    amp_own,
    ratio,
    coup_send,
    coup_recv,
    res_all,
    held_even,
    held_odd,
    margin_sem,
    b_sem,
    gat_send,
    gat_fwd,
    gat_relay,
    gat_recv,
    fit_send,
    fit_recv,
    free_sem,
):
    int_own, coup_own = amp_out, res_out
    me = lax.axis_index("pairs")
    z = lax.axis_index("fit")
    chips = n_pairs // 2
    chip, core = me // 2, lax.rem(me, 2)
    sibling = chip * 2 + (1 - core)
    pair_dev, width, _ = start_ref.shape
    per_pair = margins.shape[1]
    own_pairs = pair_dev // n_fit
    tail, fold, tail_rows = tail_shape(width)
    bands = per_pair * tail // LANES
    per_band = LANES // tail
    gathered = Parts(gathered_pairs, own_pairs)

    def margin_copy(row):
        return pltpu.make_async_copy(
            margins_ref.at[row], margins.at[row], margin_sem.at[row]
        )

    tiles = b_first_ref.shape[2] // LANES
    held = unfolded if b_hold.shape[0] == 1 else b_hold

    def b_copy(which, tile):
        return pltpu.make_async_copy(
            (b_first_ref, b_second_ref)[which].at[:, :, pl.ds(tile * LANES, LANES)],
            held.at[pl.ds((which * tiles + tile) * pair_dev, pair_dev)],
            b_sem.at[which, tile],
        )

    for tile in range(tiles):
        b_copy(0, tile).start()
        b_copy(1, tile).start()
    for row in range(pair_dev):
        margin_copy(row).start()

    barrier = pltpu.get_barrier_semaphore()

    def same_core(step):
        return lax.rem(chip + step, chips) * 2 + core

    def part_at(step):
        if n_fit & (n_fit - 1):
            return lax.rem(2 * n_fit - z - step, n_fit)
        return flip(z, step, n_fit)

    def greet(sem):
        @pl.loop(1, chips)
        def _(step):
            pl.semaphore_signal(
                sem, inc=1, device_id={"pairs": same_core(step), "fit": z}
            )

        pl.semaphore_signal(sem, inc=1, device_id={"pairs": sibling, "fit": z})
        for step in range(1, n_fit):
            pl.semaphore_signal(
                sem,
                inc=1,
                device_id={"pairs": me, "fit": part_at(step)},
            )

    greeted = chips - 1 + 1 + n_fit - 1
    greet(barrier)

    def pack_block(ref, block):
        ref[pl.ds(0, width), :] = block[:, :LANES].astype(BF16)
        pieces = []
        for part in range(fold):
            low, high = part * tail_rows, min((part + 1) * tail_rows, width)
            piece = block[low:high, LANES:]
            if high - low < tail_rows:
                filler = jnp.zeros((tail_rows - (high - low), tail), block.dtype)
                piece = jnp.concatenate([piece, filler], axis=0)
            pieces.append(piece)
        ref[pl.ds(width, tail_rows), :] = jnp.concatenate(pieces, axis=1).astype(BF16)

    def unpack_block(ref):
        main = ref[pl.ds(0, width), :].astype(F32)
        lanes = ref[pl.ds(width, tail_rows), :].astype(F32)
        pieces = []
        for part in range(fold):
            rows = min(tail_rows, width - part * tail_rows)
            pieces.append(lanes[:rows, part * tail : (part + 1) * tail])
        return jnp.concatenate([main, jnp.concatenate(pieces, axis=0)], axis=1)

    def pack(ref, blocks):
        for index, block in enumerate(blocks):
            pack_block(ref.at[index], block)

    def unpack(ref, index):
        return unpack_block(ref.at[index])

    rows_at = lax.broadcasted_iota(jnp.int32, (width, width), 0)
    cols_at = lax.broadcasted_iota(jnp.int32, (width, width), 1)

    def mask_of(row):
        count = count_ref[row]
        keep = (rows_at < count).astype(F32) * (cols_at < count).astype(F32)
        return keep

    orbitals = lax.broadcasted_iota(jnp.int32, occ_ref.shape, 1)

    def occ_of(orbital):
        return jnp.sum(
            jnp.where(orbitals == orbital, occ_ref[...], 0.0), axis=1, keepdims=True
        )

    def denominator_of(row):
        across = jnp.broadcast_to(energy_ref[pl.ds(row, 1), :], (width, width))
        down = jnp.sum(
            jnp.where(rows_at == cols_at, across, 0.0), axis=1, keepdims=True
        )
        return down + across - (occ_of(list_ref[0, row]) + occ_of(list_ref[1, row]))

    @pl.loop(0, n_fit)
    def _(part):
        pack(
            gathered.at[me * n_fit + part],
            [
                mask_of(part * own_pairs + index) * start_ref[part * own_pairs + index]
                for index in range(own_pairs)
            ],
        )

    pl.semaphore_wait(barrier, greeted)

    def direct(owner, part, step, target):
        slot = owner * n_fit + part
        return pltpu.make_async_remote_copy(
            src_ref=gathered.at[slot],
            dst_ref=gathered.at[slot],
            send_sem=gat_send.at[step, part],
            recv_sem=gat_recv.at[slot],
            device_id={"pairs": target, "fit": z},
        )

    def forward(owner, part):
        slot = owner * n_fit + part
        return pltpu.make_async_remote_copy(
            src_ref=gathered.at[slot],
            dst_ref=gathered.at[slot],
            send_sem=gat_fwd.at[slot],
            recv_sem=gat_recv.at[slot],
            device_id={"pairs": sibling, "fit": z},
        )

    relayed = chips == 4
    near = (1, 2) if relayed else ()

    def at_chip(step):
        return flip(chip, step, chips) * 2 + core

    def relay(owner, part, step):
        slot = owner * n_fit + part
        return pltpu.make_async_remote_copy(
            src_ref=gathered.at[slot],
            dst_ref=gathered.at[slot],
            send_sem=gat_relay.at[slot],
            recv_sem=gat_recv.at[slot],
            device_id={"pairs": at_chip(step), "fit": z},
        )

    def send_part(part):
        if relayed:
            for step in near:
                direct(me, part, step, at_chip(step)).start()
        else:

            @pl.loop(1, chips)
            def _(step):
                direct(me, part, step, same_core(step)).start()

        forward(me, part).start()

    def fill():
        @pl.loop(0, unfolded.shape[0] // BATCH)
        def _(batch):
            for index in range(BATCH):
                slot = batch * BATCH + index
                lanes = gathered_pairs[slot, pl.ds(width, tail_rows), :]
                for part in range(fold):
                    rows = min(tail_rows, width - part * tail_rows)
                    piece = lanes[:rows]
                    if part:
                        at = part * tail
                        piece = jnp.concatenate([piece[:, at:], piece[:, :at]], axis=1)
                    unfolded[slot, pl.ds(part * tail_rows, rows), :] = piece

    def take_direct(turn):
        part = part_at(turn)
        if relayed:
            for step in near:
                owner = at_chip(step)
                direct(owner, part, step, me).wait_recv()
                if step - 1 == turn % 2:
                    relay(owner, part, 3 - step).start()
                forward(owner, part).start()
        else:

            @pl.loop(1, chips)
            def _(step):
                owner = same_core(chips - step)
                direct(owner, part, step, me).wait_recv()
                forward(owner, part).start()

    def take_far(turn):
        part = part_at(turn)
        if relayed:
            owner = at_chip(3)
            direct(owner, part, 1, me).wait_recv()
            forward(owner, part).start()

    def take_sibling():
        @pl.loop(0, n_fit)
        def _(turn):
            part = part_at(turn)

            @pl.loop(0, chips)
            def _(step):
                owner = lax.rem(chip + chips - step, chips) * 2 + (1 - core)
                forward(owner, part).wait_recv()

        fill()

    def finish_sends():
        if relayed:
            for turn in range(n_fit):
                part = part_at(turn)
                for step in near:
                    direct(me, part, step, at_chip(step)).wait_send()
                    if step - 1 == turn % 2:
                        relay(at_chip(step), part, 3 - step).wait_send()

        @pl.loop(0, n_fit)
        def _(part):
            @pl.loop(1, chips)
            def _(step):
                if not relayed:
                    direct(me, part, step, same_core(step)).wait_send()
                forward(same_core(step), part).wait_send()

            forward(me, part).wait_send()

    def fit_copy(kind, step, index, source, target_ref):
        return pltpu.make_async_remote_copy(
            src_ref=source,
            dst_ref=target_ref,
            send_sem=fit_send.at[kind, step, index],
            recv_sem=fit_recv.at[kind, step, index],
            device_id={"pairs": me, "fit": part_at(step)},
        )

    def scatter_copy(iteration, step, index):
        return fit_copy(
            iteration,
            step,
            index,
            coup_send.at[iteration, step, index],
            coup_recv.at[iteration, step, index],
        )

    def high_copy(step, slot):
        return fit_copy(HIGH, step, 0, gathered.at[slot], gathered.at[slot])

    def res_copy(step, part, index):
        ref = res_all.at[part, index]
        return fit_copy(RES, step, index, ref, ref)

    ends_at = per_pair * LANES

    def inner_products(row, held):
        for col in range(per_pair):
            partner = partner_ref[row, col]
            amplitudes = jnp.concatenate(
                [gathered_pairs[partner, pl.ds(0, width), :], unfolded[partner]],
                axis=1,
            )
            margin = jnp.concatenate(
                [margins[row, col, :, pl.ds(0, LANES)], edge[row, col]], axis=1
            )
            product = lax.dot_general(
                amplitudes,
                margin,
                (((1,), (1,)), ((), ())),
                preferred_element_type=F32,
            )
            product = (product * fock_ref[row, col]).astype(BF16)
            held[pl.ds(col * LANES, LANES), :] = product[:LANES]
            held[pl.ds(ends_at + col * tail, tail), :] = product[LANES:]

    def outer_products(row, held):
        wide = jnp.concatenate(
            [margins[row, col, :, pl.ds(0, LANES)] for col in range(per_pair)]
            + [band[row, part] for part in range(bands)],
            axis=1,
        )
        return jnp.dot(wide, held[...], preferred_element_type=F32)

    def row_at(turn):
        step = n_fit - 1 - (turn % n_fit)
        return part_at(step) * own_pairs + turn // n_fit

    def couple_all(action):
        if held_odd.shape != held_even.shape:

            @pl.loop(0, pair_dev)
            def _(turn):
                inner_products(row_at(turn), held_even)
                action(turn, outer_products(row_at(turn), held_even))

            return
        inner_products(row_at(0), held_even)

        def two_rows(turn, more):
            coupling = outer_products(row_at(turn), held_even)
            inner_products(row_at(turn + 1), held_odd)
            action(turn, coupling)
            coupling = outer_products(row_at(turn + 1), held_odd)
            if more:
                inner_products(row_at(turn + 2), held_even)
            action(turn + 1, coupling)

        @pl.loop(0, pair_dev // 2 - 1)
        def _(step):
            two_rows(2 * step, True)

        two_rows(pair_dev - 2, False)

    HIGH, RES = ITERS, ITERS + 1

    def partial_of(iteration, row):
        return coup_own[row] if iteration else coup_own[row] - int_own[row]


    @pl.loop(0, n_fit)
    def _(part):
        send_part(part_at(part))

    for tile in range(tiles):
        b_copy(0, tile).wait()
        b_copy(1, tile).wait()

    def b_row(which, row):
        return jnp.concatenate(
            [held[(which * tiles + tile) * pair_dev + row] for tile in range(tiles)],
            axis=1,
        )

    def integrals_of(row):
        return lax.dot_general(
            b_row(0, row),
            b_row(1, row),
            (((1,), (1,)), ((), ())),
            preferred_element_type=F32,
        )

    def prepare(row):
        int_own[row] = integrals_of(row)
        ratio[row] = mask_of(row) / denominator_of(row)
        margin_copy(row).wait()
        blank = jnp.zeros((width, LANES - tail), BF16)

        @pl.loop(0, bands)
        def _(part):
            pieces = []
            for index in range(per_band):
                col = part * per_band + index
                piece = margins[row, col][:, LANES:]
                edge[row, col] = jnp.concatenate([piece, blank], axis=1)
                pieces.append(piece)
            band[row, part] = jnp.concatenate(pieces, axis=1)

    for turn in range(n_fit):

        @pl.loop(turn * own_pairs, (turn + 1) * own_pairs)
        def _(row):
            prepare(row)

        take_direct(turn)
    for turn in range(n_fit):
        take_far(turn)
    take_sibling()

    def finish(iteration, index):
        row = z * own_pairs + index
        total = partial_of(iteration, row)
        for turn in range(1, n_fit):
            step = n_fit - turn
            scatter_copy(iteration, step, index).wait()
            total = total + unpack_block(coup_recv.at[iteration, step, index])
        if iteration == 0:
            amp_own[index] = total * ratio[row]
        else:
            pack_block(res_all.at[z, index], mask_of(row) * total)
            for step in range(1, n_fit):
                res_copy(step, z, index).start()

    for iteration in range(ITERS):

        def after_row(turn, coupling):
            index = turn // n_fit
            step = n_fit - 1 - (turn % n_fit)
            row = row_at(turn)
            coup_own[row] = coup_own[row] - coupling if iteration else coupling

            @pl.when(step > 0)
            def _():
                pack_block(
                    coup_send.at[iteration, step, index], partial_of(iteration, row)
                )
                scatter_copy(iteration, step, index).start()

        couple_all(after_row)

        if iteration < ITERS - 1:
            finish_sends()
            greet(free_sem)
            for index in range(own_pairs):
                finish(iteration, index)
            pl.semaphore_wait(free_sem, greeted)
            mine = me * n_fit + z
            pack(gathered.at[mine], [amp_own[index] for index in range(own_pairs)])
            for step in range(1, n_fit):
                high_copy(step, mine).start()
            send_part(z)
            for turn in range(1, n_fit):
                part = part_at(turn)
                high_copy(turn, me * n_fit + part).wait_recv()
                send_part(part)
                take_direct(turn - 1)
                if turn > 1:
                    take_far(turn - 2)
            take_direct(n_fit - 1)
            for turn in range(max(n_fit - 2, 0), n_fit):
                take_far(turn)
            take_sibling()
            for step in range(1, n_fit):
                high_copy(step, mine).wait_send()
        else:
            for index in range(own_pairs):
                finish(iteration, index)

    finish_sends()

    @pl.loop(0, pair_dev)
    def _(turn):
        index, step = turn // n_fit, (turn % n_fit)
        part = part_at(step)

        @pl.when(step > 0)
        def _():
            res_copy(step, part, index).wait_recv()

        row = part * own_pairs + index
        residual = unpack_block(res_all.at[part, index])
        amplitudes = unpack(gathered.at[me * n_fit + part], index)
        res_out[row] = residual
        amp_out[row] = amplitudes - residual * ratio[row]

    for index in range(own_pairs):
        for step in range(1, n_fit):
            res_copy(step, z, index).wait_send()


def shards(
    n_pairs,
    n_fit,
    b_first,
    b_second,
    start_amplitudes,
    margins,
    fock_terms,
    partners,
    pno_energy,
    occ_energy,
    pair_list,
    pno_count,
):
    pair_dev, width, _ = start_amplitudes.shape
    own_pairs = pair_dev // n_fit
    per_pair = margins.shape[1]
    tail, _, tail_rows = tail_shape(width)
    block = (width + tail_rows, LANES)
    packed = (own_pairs,) + block
    slots = n_pairs * n_fit
    b_slots = 2 * pair_dev * b_first.shape[2] // LANES
    if b_slots <= n_pairs * pair_dev:
        b_slots = 1
    out = jax.ShapeDtypeStruct(start_amplitudes.shape, F32)
    vmem = pl.BlockSpec(memory_space=pltpu.VMEM)
    smem = pl.BlockSpec(memory_space=pltpu.SMEM)
    hbm = pl.BlockSpec(memory_space=pl.ANY)
    return pl.pallas_call(
        functools.partial(kernel, n_pairs, n_fit),
        out_shape=(out, out),
        in_specs=[vmem, vmem, smem, smem, vmem, smem, smem, hbm, hbm, hbm],
        out_specs=(vmem, vmem),
        scratch_shapes=[
            pltpu.VMEM(margins.shape, BF16),
            pltpu.VMEM((pair_dev, per_pair, width, LANES), BF16),
            pltpu.VMEM((pair_dev, per_pair * tail // LANES, width, LANES), BF16),
            pltpu.VMEM((b_slots, width, LANES), BF16),
            pltpu.VMEM((n_pairs * pair_dev,) + block, BF16),
            pltpu.VMEM((n_pairs * pair_dev, width, LANES), BF16),
            pltpu.VMEM((own_pairs, width, width), F32),
            pltpu.VMEM((pair_dev, width, width), F32),
            pltpu.VMEM((ITERS, n_fit) + packed, BF16),
            pltpu.VMEM((ITERS, n_fit) + packed, BF16),
            pltpu.VMEM((n_fit,) + packed, BF16),
            pltpu.VMEM((per_pair * width, width), BF16),
            pltpu.VMEM((per_pair * width if n_pairs == 8 else SUBLANES, width), BF16),
            pltpu.SemaphoreType.DMA((pair_dev,)),
            pltpu.SemaphoreType.DMA((2, b_first.shape[2] // LANES)),
            pltpu.SemaphoreType.DMA((n_pairs // 2, n_fit)),
            pltpu.SemaphoreType.DMA((slots,)),
            pltpu.SemaphoreType.DMA((slots,)),
            pltpu.SemaphoreType.DMA((slots,)),
            pltpu.SemaphoreType.DMA((ITERS + 2, n_fit, own_pairs)),
            pltpu.SemaphoreType.DMA((ITERS + 2, n_fit, own_pairs)),
            pltpu.SemaphoreType.REGULAR,
        ],
        compiler_params=pltpu.CompilerParams(
            collective_id=0, has_side_effects=True, vmem_limit_bytes=65000 * 1024
        ),
    )(
        start_amplitudes,
        pno_energy,
        fock_terms,
        partners,
        occ_energy.reshape(1, -1),
        pair_list.T,
        pno_count,
        b_first,
        b_second,
        margins,
    )


def solution(mesh):
    return jax.shard_map(
        functools.partial(shards, mesh.shape["pairs"], mesh.shape["fit"]),
        mesh=mesh,
        in_specs=(
            P("pairs", None, "fit"),
            P("pairs", None, "fit"),
            P("pairs", None, None),
            P("pairs", "fit", None, None),
            P("pairs", "fit"),
            P("pairs", "fit"),
            P("pairs", None),
            P(),
            P("pairs", None),
            P("pairs"),
        ),
        out_specs=(P("pairs", None, None), P("pairs", None, None)),
        check_vma=False,
    )
```

```python
import functools
import jax
import jax.numpy as jnp
from jax import lax
from jax.experimental import pallas as pl
from jax.experimental.pallas import tpu as pltpu
from jax.sharding import PartitionSpec as P

ITERS = 2
LANES = 128
SUBLANES = 16
BATCH = 8
BF16 = jnp.bfloat16
F32 = jnp.float32


def flip(value, bits, size):
    result, place = 0, 1
    while place < size:
        one = (value // place) % 2
        other = (bits // place) % 2
        result = result + place * ((one + other) % 2)
        place *= 2
    return result


def tail_shape(width):
    tail = width - LANES
    fold = LANES // tail
    rows = -(-width // (fold * SUBLANES)) * SUBLANES
    return tail, fold, rows


class Parts:
    def __init__(self, ref, size):
        self.ref, self.size, self.at = ref, size, self

    def __getitem__(self, slot):
        return self.ref.at[pl.ds(slot * self.size, self.size)]


def kernel(
    n_pairs,
    n_fit,
    start_ref,
    energy_ref,
    fock_ref,
    partner_ref,
    occ_ref,
    list_ref,
    count_ref,
    b_first_ref,
    b_second_ref,
    margins_ref,
    amp_result,
    res_result,
    amp_out,
    res_out,
    margins,
    edge,
    band,
    b_hold,
    gathered_pairs,
    unfolded,
    amp_own,
    ratio,
    coup_send,
    coup_recv,
    res_all,
    held_even,
    held_odd,
    out_sem,
    margin_sem,
    b_sem,
    gat_send,
    gat_fwd,
    gat_relay,
    gat_recv,
    fit_send,
    fit_recv,
    free_sem,
):
    int_own, coup_own = amp_out, res_out
    me = lax.axis_index("pairs")
    z = lax.axis_index("fit")
    chips = n_pairs // 2
    chip, core = me // 2, lax.rem(me, 2)
    sibling = chip * 2 + (1 - core)
    pair_dev, width, _ = start_ref.shape
    per_pair = margins.shape[1]
    own_pairs = pair_dev // n_fit
    tail, fold, tail_rows = tail_shape(width)
    bands = per_pair * tail // LANES
    per_band = LANES // tail
    gathered = Parts(gathered_pairs, own_pairs)

    def margin_copy(row):
        return pltpu.make_async_copy(
            margins_ref.at[row], margins.at[row], margin_sem.at[row]
        )

    def result_copy(which, row):
        source, target = ((amp_out, amp_result), (res_out, res_result))[which]
        return pltpu.make_async_copy(
            source.at[row], target.at[row], out_sem.at[which, row]
        )

    tiles = b_first_ref.shape[2] // LANES
    held = unfolded if b_hold.shape[0] == 1 else b_hold

    def b_copy(which, tile):
        return pltpu.make_async_copy(
            (b_first_ref, b_second_ref)[which].at[:, :, pl.ds(tile * LANES, LANES)],
            held.at[pl.ds((which * tiles + tile) * pair_dev, pair_dev)],
            b_sem.at[which, tile],
        )

    for tile in range(tiles):
        b_copy(0, tile).start()
        b_copy(1, tile).start()
    for row in range(pair_dev):
        margin_copy(row).start()

    barrier = pltpu.get_barrier_semaphore()

    def same_core(step):
        return lax.rem(chip + step, chips) * 2 + core

    def part_at(step):
        if n_fit & (n_fit - 1):
            return lax.rem(2 * n_fit - z - step, n_fit)
        return flip(z, step, n_fit)

    def greet(sem):
        @pl.loop(1, chips)
        def _(step):
            pl.semaphore_signal(
                sem, inc=1, device_id={"pairs": same_core(step), "fit": z}
            )

        pl.semaphore_signal(sem, inc=1, device_id={"pairs": sibling, "fit": z})
        for step in range(1, n_fit):
            pl.semaphore_signal(
                sem,
                inc=1,
                device_id={"pairs": me, "fit": part_at(step)},
            )

    greeted = chips - 1 + 1 + n_fit - 1
    greet(barrier)

    def pack_block(ref, block):
        ref[pl.ds(0, width), :] = block[:, :LANES].astype(BF16)
        pieces = []
        for part in range(fold):
            low, high = part * tail_rows, min((part + 1) * tail_rows, width)
            piece = block[low:high, LANES:]
            if high - low < tail_rows:
                filler = jnp.zeros((tail_rows - (high - low), tail), block.dtype)
                piece = jnp.concatenate([piece, filler], axis=0)
            pieces.append(piece)
        ref[pl.ds(width, tail_rows), :] = jnp.concatenate(pieces, axis=1).astype(BF16)

    def unpack_block(ref):
        main = ref[pl.ds(0, width), :].astype(F32)
        lanes = ref[pl.ds(width, tail_rows), :].astype(F32)
        pieces = []
        for part in range(fold):
            rows = min(tail_rows, width - part * tail_rows)
            pieces.append(lanes[:rows, part * tail : (part + 1) * tail])
        return jnp.concatenate([main, jnp.concatenate(pieces, axis=0)], axis=1)

    def pack(ref, blocks):
        for index, block in enumerate(blocks):
            pack_block(ref.at[index], block)

    def unpack(ref, index):
        return unpack_block(ref.at[index])

    rows_at = lax.broadcasted_iota(jnp.int32, (width, width), 0)
    cols_at = lax.broadcasted_iota(jnp.int32, (width, width), 1)

    def mask_of(row):
        count = count_ref[row]
        keep = (rows_at < count).astype(F32) * (cols_at < count).astype(F32)
        return keep

    orbitals = lax.broadcasted_iota(jnp.int32, occ_ref.shape, 1)

    def occ_of(orbital):
        return jnp.sum(
            jnp.where(orbitals == orbital, occ_ref[...], 0.0), axis=1, keepdims=True
        )

    def denominator_of(row):
        across = jnp.broadcast_to(energy_ref[pl.ds(row, 1), :], (width, width))
        down = jnp.sum(
            jnp.where(rows_at == cols_at, across, 0.0), axis=1, keepdims=True
        )
        return down + across - (occ_of(list_ref[0, row]) + occ_of(list_ref[1, row]))

    @pl.loop(0, n_fit)
    def _(part):
        pack(
            gathered.at[me * n_fit + part],
            [
                mask_of(part * own_pairs + index) * start_ref[part * own_pairs + index]
                for index in range(own_pairs)
            ],
        )

    pl.semaphore_wait(barrier, greeted)

    def direct(owner, part, step, target):
        slot = owner * n_fit + part
        return pltpu.make_async_remote_copy(
            src_ref=gathered.at[slot],
            dst_ref=gathered.at[slot],
            send_sem=gat_send.at[step, part],
            recv_sem=gat_recv.at[slot],
            device_id={"pairs": target, "fit": z},
        )

    def forward(owner, part):
        slot = owner * n_fit + part
        return pltpu.make_async_remote_copy(
            src_ref=gathered.at[slot],
            dst_ref=gathered.at[slot],
            send_sem=gat_fwd.at[slot],
            recv_sem=gat_recv.at[slot],
            device_id={"pairs": sibling, "fit": z},
        )

    relayed = chips == 4
    near = (1, 2) if relayed else ()

    def at_chip(step):
        return flip(chip, step, chips) * 2 + core

    def relay(owner, part, step):
        slot = owner * n_fit + part
        return pltpu.make_async_remote_copy(
            src_ref=gathered.at[slot],
            dst_ref=gathered.at[slot],
            send_sem=gat_relay.at[slot],
            recv_sem=gat_recv.at[slot],
            device_id={"pairs": at_chip(step), "fit": z},
        )

    def send_part(part):
        if relayed:
            for step in near:
                direct(me, part, step, at_chip(step)).start()
        else:

            @pl.loop(1, chips)
            def _(step):
                direct(me, part, step, same_core(step)).start()

        forward(me, part).start()

    def fill():
        @pl.loop(0, unfolded.shape[0] // BATCH)
        def _(batch):
            for index in range(BATCH):
                slot = batch * BATCH + index
                lanes = gathered_pairs[slot, pl.ds(width, tail_rows), :]
                for part in range(fold):
                    rows = min(tail_rows, width - part * tail_rows)
                    piece = lanes[:rows]
                    if part:
                        at = part * tail
                        piece = jnp.concatenate([piece[:, at:], piece[:, :at]], axis=1)
                    unfolded[slot, pl.ds(part * tail_rows, rows), :] = piece

    def take_direct(turn):
        part = part_at(turn)
        if relayed:
            for step in near:
                owner = at_chip(step)
                direct(owner, part, step, me).wait_recv()
                if step - 1 == turn % 2:
                    relay(owner, part, 3 - step).start()
                forward(owner, part).start()
        else:

            @pl.loop(1, chips)
            def _(step):
                owner = same_core(chips - step)
                direct(owner, part, step, me).wait_recv()
                forward(owner, part).start()

    def take_far(turn):
        part = part_at(turn)
        if relayed:
            owner = at_chip(3)
            direct(owner, part, 1, me).wait_recv()
            forward(owner, part).start()

    def take_sibling():
        @pl.loop(0, n_fit)
        def _(turn):
            part = part_at(turn)

            @pl.loop(0, chips)
            def _(step):
                owner = lax.rem(chip + chips - step, chips) * 2 + (1 - core)
                forward(owner, part).wait_recv()

        fill()

    def finish_sends():
        if relayed:
            for turn in range(n_fit):
                part = part_at(turn)
                for step in near:
                    direct(me, part, step, at_chip(step)).wait_send()
                    if step - 1 == turn % 2:
                        relay(at_chip(step), part, 3 - step).wait_send()

        @pl.loop(0, n_fit)
        def _(part):
            @pl.loop(1, chips)
            def _(step):
                if not relayed:
                    direct(me, part, step, same_core(step)).wait_send()
                forward(same_core(step), part).wait_send()

            forward(me, part).wait_send()

    def fit_copy(kind, step, index, source, target_ref):
        return pltpu.make_async_remote_copy(
            src_ref=source,
            dst_ref=target_ref,
            send_sem=fit_send.at[kind, step, index],
            recv_sem=fit_recv.at[kind, step, index],
            device_id={"pairs": me, "fit": part_at(step)},
        )

    def scatter_copy(iteration, step, index):
        return fit_copy(
            iteration,
            step,
            index,
            coup_send.at[iteration, step, index],
            coup_recv.at[iteration, step, index],
        )

    def high_copy(step, slot):
        return fit_copy(HIGH, step, 0, gathered.at[slot], gathered.at[slot])

    def res_copy(step, part, index):
        ref = res_all.at[part, index]
        return fit_copy(RES, step, index, ref, ref)

    ends_at = per_pair * LANES

    def inner_products(row, held):
        for col in range(per_pair):
            partner = partner_ref[row, col]
            amplitudes = jnp.concatenate(
                [gathered_pairs[partner, pl.ds(0, width), :], unfolded[partner]],
                axis=1,
            )
            margin = jnp.concatenate(
                [margins[row, col, :, pl.ds(0, LANES)], edge[row, col]], axis=1
            )
            product = lax.dot_general(
                amplitudes,
                margin,
                (((1,), (1,)), ((), ())),
                preferred_element_type=F32,
            )
            product = (product * fock_ref[row, col]).astype(BF16)
            held[pl.ds(col * LANES, LANES), :] = product[:LANES]
            held[pl.ds(ends_at + col * tail, tail), :] = product[LANES:]

    def outer_products(row, held):
        wide = jnp.concatenate(
            [margins[row, col, :, pl.ds(0, LANES)] for col in range(per_pair)]
            + [band[row, part] for part in range(bands)],
            axis=1,
        )
        return jnp.dot(wide, held[...], preferred_element_type=F32)

    def row_at(turn):
        step = n_fit - 1 - (turn % n_fit)
        return part_at(step) * own_pairs + turn // n_fit

    def couple_all(action):
        if held_odd.shape != held_even.shape:

            @pl.loop(0, pair_dev)
            def _(turn):
                inner_products(row_at(turn), held_even)
                action(turn, outer_products(row_at(turn), held_even))

            return
        inner_products(row_at(0), held_even)

        def two_rows(turn, more):
            coupling = outer_products(row_at(turn), held_even)
            inner_products(row_at(turn + 1), held_odd)
            action(turn, coupling)
            coupling = outer_products(row_at(turn + 1), held_odd)
            if more:
                inner_products(row_at(turn + 2), held_even)
            action(turn + 1, coupling)

        @pl.loop(0, pair_dev // 2 - 1)
        def _(step):
            two_rows(2 * step, True)

        two_rows(pair_dev - 2, False)

    HIGH, RES = ITERS, ITERS + 1

    def partial_of(iteration, row):
        return coup_own[row] if iteration else coup_own[row] - int_own[row]


    @pl.loop(0, n_fit)
    def _(part):
        send_part(part_at(part))

    for tile in range(tiles):
        b_copy(0, tile).wait()
        b_copy(1, tile).wait()

    def b_row(which, row):
        return jnp.concatenate(
            [held[(which * tiles + tile) * pair_dev + row] for tile in range(tiles)],
            axis=1,
        )

    def integrals_of(row):
        return lax.dot_general(
            b_row(0, row),
            b_row(1, row),
            (((1,), (1,)), ((), ())),
            preferred_element_type=F32,
        )

    def prepare(row):
        int_own[row] = integrals_of(row)
        ratio[row] = mask_of(row) / denominator_of(row)
        margin_copy(row).wait()
        blank = jnp.zeros((width, LANES - tail), BF16)

        @pl.loop(0, bands)
        def _(part):
            pieces = []
            for index in range(per_band):
                col = part * per_band + index
                piece = margins[row, col][:, LANES:]
                edge[row, col] = jnp.concatenate([piece, blank], axis=1)
                pieces.append(piece)
            band[row, part] = jnp.concatenate(pieces, axis=1)

    for turn in range(n_fit):

        @pl.loop(turn * own_pairs, (turn + 1) * own_pairs)
        def _(row):
            prepare(row)

        take_direct(turn)
    for turn in range(n_fit):
        take_far(turn)
    take_sibling()

    def finish(iteration, index):
        row = z * own_pairs + index
        total = partial_of(iteration, row)
        for turn in range(1, n_fit):
            step = n_fit - turn
            scatter_copy(iteration, step, index).wait()
            total = total + unpack_block(coup_recv.at[iteration, step, index])
        if iteration == 0:
            amp_own[index] = total * ratio[row]
        else:
            pack_block(res_all.at[z, index], mask_of(row) * total)
            for step in range(1, n_fit):
                res_copy(step, z, index).start()

    for iteration in range(ITERS):

        def after_row(turn, coupling):
            index = turn // n_fit
            step = n_fit - 1 - (turn % n_fit)
            row = row_at(turn)
            coup_own[row] = coup_own[row] - coupling if iteration else coupling

            @pl.when(step > 0)
            def _():
                pack_block(
                    coup_send.at[iteration, step, index], partial_of(iteration, row)
                )
                scatter_copy(iteration, step, index).start()

        couple_all(after_row)

        if iteration < ITERS - 1:
            finish_sends()
            greet(free_sem)
            for index in range(own_pairs):
                finish(iteration, index)
            pl.semaphore_wait(free_sem, greeted)
            mine = me * n_fit + z
            pack(gathered.at[mine], [amp_own[index] for index in range(own_pairs)])
            for step in range(1, n_fit):
                high_copy(step, mine).start()
            send_part(z)
            for turn in range(1, n_fit):
                part = part_at(turn)
                high_copy(turn, me * n_fit + part).wait_recv()
                send_part(part)
                take_direct(turn - 1)
                if turn > 1:
                    take_far(turn - 2)
            take_direct(n_fit - 1)
            for turn in range(max(n_fit - 2, 0), n_fit):
                take_far(turn)
            take_sibling()
            for step in range(1, n_fit):
                high_copy(step, mine).wait_send()
        else:
            for index in range(own_pairs):
                finish(iteration, index)

    finish_sends()

    @pl.loop(0, pair_dev)
    def _(turn):
        index, step = turn // n_fit, (turn % n_fit)
        part = part_at(step)

        @pl.when(step > 0)
        def _():
            res_copy(step, part, index).wait_recv()

        row = part * own_pairs + index
        residual = unpack_block(res_all.at[part, index])
        amplitudes = unpack(gathered.at[me * n_fit + part], index)
        res_out[row] = residual
        amp_out[row] = amplitudes - residual * ratio[row]
        result_copy(0, row).start()
        result_copy(1, row).start()

    for row in range(pair_dev):
        result_copy(0, row).wait()
        result_copy(1, row).wait()

    for index in range(own_pairs):
        for step in range(1, n_fit):
            res_copy(step, z, index).wait_send()


def shards(
    n_pairs,
    n_fit,
    b_first,
    b_second,
    start_amplitudes,
    margins,
    fock_terms,
    partners,
    pno_energy,
    occ_energy,
    pair_list,
    pno_count,
):
    pair_dev, width, _ = start_amplitudes.shape
    own_pairs = pair_dev // n_fit
    per_pair = margins.shape[1]
    tail, _, tail_rows = tail_shape(width)
    block = (width + tail_rows, LANES)
    packed = (own_pairs,) + block
    slots = n_pairs * n_fit
    b_slots = 2 * pair_dev * b_first.shape[2] // LANES
    if b_slots <= n_pairs * pair_dev:
        b_slots = 1
    out = jax.ShapeDtypeStruct(start_amplitudes.shape, F32)
    vmem = pl.BlockSpec(memory_space=pltpu.VMEM)
    smem = pl.BlockSpec(memory_space=pltpu.SMEM)
    hbm = pl.BlockSpec(memory_space=pl.ANY)
    return pl.pallas_call(
        functools.partial(kernel, n_pairs, n_fit),
        out_shape=(out, out),
        in_specs=[vmem, vmem, smem, smem, vmem, smem, smem, hbm, hbm, hbm],
        out_specs=(hbm, hbm),
        scratch_shapes=[
            pltpu.VMEM(start_amplitudes.shape, F32),
            pltpu.VMEM(start_amplitudes.shape, F32),
            pltpu.VMEM(margins.shape, BF16),
            pltpu.VMEM((pair_dev, per_pair, width, LANES), BF16),
            pltpu.VMEM((pair_dev, per_pair * tail // LANES, width, LANES), BF16),
            pltpu.VMEM((b_slots, width, LANES), BF16),
            pltpu.VMEM((n_pairs * pair_dev,) + block, BF16),
            pltpu.VMEM((n_pairs * pair_dev, width, LANES), BF16),
            pltpu.VMEM((own_pairs, width, width), F32),
            pltpu.VMEM((pair_dev, width, width), F32),
            pltpu.VMEM((ITERS, n_fit) + packed, BF16),
            pltpu.VMEM((ITERS, n_fit) + packed, BF16),
            pltpu.VMEM((n_fit,) + packed, BF16),
            pltpu.VMEM((per_pair * width, width), BF16),
            pltpu.VMEM((per_pair * width if n_pairs == 8 else SUBLANES, width), BF16),
            pltpu.SemaphoreType.DMA((2, pair_dev)),
            pltpu.SemaphoreType.DMA((pair_dev,)),
            pltpu.SemaphoreType.DMA((2, b_first.shape[2] // LANES)),
            pltpu.SemaphoreType.DMA((n_pairs // 2, n_fit)),
            pltpu.SemaphoreType.DMA((slots,)),
            pltpu.SemaphoreType.DMA((slots,)),
            pltpu.SemaphoreType.DMA((slots,)),
            pltpu.SemaphoreType.DMA((ITERS + 2, n_fit, own_pairs)),
            pltpu.SemaphoreType.DMA((ITERS + 2, n_fit, own_pairs)),
            pltpu.SemaphoreType.REGULAR,
        ],
        compiler_params=pltpu.CompilerParams(
            collective_id=0, has_side_effects=True, vmem_limit_bytes=65000 * 1024
        ),
    )(
        start_amplitudes,
        pno_energy,
        fock_terms,
        partners,
        occ_energy.reshape(1, -1),
        pair_list.T,
        pno_count,
        b_first,
        b_second,
        margins,
    )


def solution(mesh):
    return jax.shard_map(
        functools.partial(shards, mesh.shape["pairs"], mesh.shape["fit"]),
        mesh=mesh,
        in_specs=(
            P("pairs", None, "fit"),
            P("pairs", None, "fit"),
            P("pairs", None, None),
            P("pairs", "fit", None, None),
            P("pairs", "fit"),
            P("pairs", "fit"),
            P("pairs", None),
            P(),
            P("pairs", None),
            P("pairs"),
        ),
        out_specs=(P("pairs", None, None), P("pairs", None, None)),
        check_vma=False,
    )
```
